128 devices in a mesh: vox: 16 (over y, x), dir: 8 (over z, core).
Axes of the slice: x: 4, y: 4, z: 4, core: 2. Of those that a mesh axis runs over, the one named last changes fastest.
Arguments:
- signal: bfloat16 [1200, 262144], P('dir', 'vox'), may hold values from -6 to 6
- response: bfloat16 [153, 1200], replicated, may hold values from -0.1875 to 0.1875
- sphere_basis: bfloat16 [1200, 153], replicated, may hold values from -0.5 to 0.5
- initial: float32 [153, 262144], P(None, ('vox', 'dir')), may hold values from -6 to 6
- similarity: bfloat16 [2048, 27, 128, 128], P(('vox', 'dir')), may hold values from 0.0009994507 to 1
- neighbour_count: int32 [2048], P(('vox', 'dir')), may hold values from 1 to 27
- neighbour_index: int32 [2048, 27], P(('vox', 'dir')), may hold values from 0 to 63, as said below
- fetch_list: int32 [128, 16, 3], P(('vox', 'dir')), may hold values from 0 to 15
Outputs:
- coefficients: float32 [153, 262144], P(None, ('vox', 'dir'))
The draws below stay inside these ranges and needn't reach their ends.
Inputs may be any that keep to these rules, and one draw needn't show every extreme that they name: `neighbour_index`: the 27 entries of one row are distinct.
All inputs are finite; a program needn't handle non-finite values.
Results may differ from the reference program's by a relative error of at most 0.00033.
Values may be sent and summed in bfloat16 or wider, within the bound.
No kernel may reach another device: no remote copies, remote signals or barrier semaphores. Data moves between devices by JAX's collectives and lax.ppermute only.
A program may use at most 128 MiB of HBM per device.

```python
import math
import jax
import jax.numpy as jnp
from jax import lax

K = 153
G = 1200
NS = 1200
BS = 128
MAXNB = 27
CAP = 3
ITERS = 3
BLK_DEV = 16
VOX_DEV = 2048
NBLK = 2048
VOXELS = 262144
CANDS = 64
N_VOX = 16
N_DIR = 8


def draw_neighbour_index(key, part):
    scores = jax.random.randint(key, (NBLK, CANDS), 0, 1048576, dtype=jnp.int32)
    scores = scores * CANDS + jnp.arange(CANDS, dtype=jnp.int32)[None, :]
    order_rows = jnp.argsort(scores, axis=1)
    return order_rows[:, :MAXNB].astype(jnp.int32)


def set_ends(array, own_key, smallest, high):
    spot = [jax.random.randint(jax.random.fold_in(own_key, axis), (), 0, length) for axis, length in enumerate(array.shape)]
    longest = array.shape.index(max(array.shape))
    next_to = spot[:longest] + [(spot[longest] + 1) % array.shape[longest]] + spot[longest + 1:]
    return array.at[tuple(spot)].set(smallest).at[tuple(next_to)].set(high)


def levels(key, extent, split, low, largest):
    gain = 1.0
    for dim, parts in split:
        draws = jax.random.uniform(jax.random.fold_in(jax.random.fold_in(key, 6), dim), (parts,), jnp.float32, low / len(split), largest / len(split))
        gain = gain * jnp.repeat(jnp.exp(draws), extent[dim] // parts).reshape((-1,) + (1,) * (len(extent) - 1 - dim))
    return gain


def bell_draw(own_key, shape, spread, limit, split=(), kind=jnp.bfloat16):
    result = jax.random.normal(own_key, shape, jnp.float32) * spread
    if len(split) > 0:
        result = levels(own_key, shape, split, -0.22, 0.18) * result
    return jnp.clip(result, min=-limit, max=limit).astype(kind)


def setup_inputs(seed: int = 0) -> dict:
    key_of = jax.random.split(jax.random.key(seed), 9)
    signal = bell_draw(key_of[0], (G, VOXELS), 1.0, 6.0, ((0, 8), (1, 16)))
    response = bell_draw(key_of[1], (K, G), G ** -0.5, 0.1875)
    sphere_basis = bell_draw(key_of[2], (NS, K), K ** -0.5, 0.5)
    initial = bell_draw(key_of[3], (K, VOXELS), 1.0, 6.0, ((1, 128),), jnp.float32)
    similarity = jnp.clip(jnp.exp(math.log(1.0) - 6.9083047 * jax.random.uniform(key_of[4], (NBLK, MAXNB, BS, BS), jnp.float32) ** levels(key_of[4], (NBLK, MAXNB, BS, BS), ((0, 128),), -0.2, 0.2)), 0.0009994507, 1.0).astype(jnp.bfloat16)
    neighbour_count = set_ends(jax.random.randint(key_of[5], (NBLK,), 1, MAXNB + 1), jax.random.fold_in(key_of[5], 1), 1, MAXNB).astype(jnp.int32)
    neighbour_index = draw_neighbour_index(jax.random.fold_in(key_of[8], 71), 0)
    fetch_list = set_ends(jax.random.randint(key_of[7], (N_VOX * N_DIR, N_VOX, CAP), 0, BLK_DEV), jax.random.fold_in(key_of[7], 1), 0, BLK_DEV - 1).astype(jnp.int32)
    return {"signal": signal, "response": response, "sphere_basis": sphere_basis, "initial": initial, "similarity": similarity, "neighbour_count": neighbour_count, "neighbour_index": neighbour_index, "fetch_list": fetch_list}


step_size = 0.2
smooth_weight = 2.0
penalty_weight = 0.1
sparsity = 0.25


def reference(signal, response, sphere_basis, initial, similarity, neighbour_count, neighbour_index, fetch_list):
    device_count = N_VOX * N_DIR
    fitted = jnp.dot(response, signal, preferred_element_type=jnp.float32)
    gram_matrix = jnp.dot(response, response.T, preferred_element_type=jnp.float32)
    device_ids = jnp.arange(device_count, dtype=jnp.int32)
    own_ids = device_ids[:, None] * BLK_DEV + jnp.arange(BLK_DEV, dtype=jnp.int32)[None, :]
    owner_ids = jnp.arange(N_VOX, dtype=jnp.int32)[None, :] * N_DIR + (device_ids % N_DIR)[:, None]
    far_ids = (owner_ids[:, :, None] * BLK_DEV + fetch_list).reshape(device_count, N_VOX * CAP)
    cand_table = jnp.concatenate([own_ids, far_ids], axis=1).astype(jnp.int32)
    row_owner = jnp.arange(NBLK, dtype=jnp.int32) // BLK_DEV
    global_ids = jnp.take_along_axis(cand_table[row_owner], neighbour_index.astype(jnp.int32), axis=1)
    live_slot = jnp.arange(MAXNB, dtype=jnp.int32)[None, :] < neighbour_count[:, None]
    row_sums = jnp.sum(similarity, axis=3, dtype=jnp.float32)
    degree = jnp.sum(jnp.where(live_slot[:, :, None], row_sums, jnp.zeros((), row_sums.dtype)), axis=1)

    def to_devices(field):
        return field.reshape(field.shape[0], device_count, VOX_DEV).transpose(1, 0, 2)

    fitted_dev = to_devices(fitted)
    degree_dev = degree.reshape(device_count, 1, VOX_DEV)
    weights_dev = similarity.reshape(device_count, BLK_DEV, MAXNB, BS, BS)
    ids_dev = global_ids.reshape(device_count, BLK_DEV, MAXNB)
    live_dev = live_slot.reshape(device_count, BLK_DEV, MAXNB)
    coeffs = to_devices(initial)
    threshold = step_size * sparsity
    for iteration in range(ITERS):
        rounded = lax.optimization_barrier(coeffs.astype(jnp.bfloat16))
        blocks = rounded.reshape(device_count, K, BLK_DEV, BS).transpose(0, 2, 1, 3).reshape(NBLK, K, BS)

        def update(inputs):
            coeff_here, round_here, fit_here, deg_here, weight_here, id_here, live_here = inputs
            nearby = blocks[id_here].astype(jnp.float32)
            masked = jnp.where(live_here[:, :, None, None], weight_here.astype(jnp.float32), jnp.zeros((), jnp.float32))
            graph_term = jnp.einsum("rmab,rmkb->kra", masked, nearby, precision=lax.Precision.HIGHEST).reshape(K, VOX_DEV)
            amplitude = jnp.dot(sphere_basis, round_here, preferred_element_type=jnp.float32)
            negative = lax.optimization_barrier(jnp.minimum(amplitude, 0.0).astype(jnp.bfloat16))
            pulled = jnp.dot(sphere_basis.T, negative, preferred_element_type=jnp.float32)
            fidelity = jnp.dot(gram_matrix, coeff_here, precision=lax.Precision.HIGHEST, preferred_element_type=jnp.float32)
            gradient = fidelity - fit_here + smooth_weight * (coeff_here - graph_term / deg_here) + penalty_weight * pulled
            stepped = coeff_here - step_size * gradient
            return stepped - jnp.clip(stepped, -threshold, threshold)

        coeffs = lax.map(update, (coeffs, rounded, fitted_dev, degree_dev, weights_dev, ids_dev, live_dev))
    return coeffs.transpose(1, 0, 2).reshape(K, VOXELS)
```

```python
import jax
import jax.numpy as jnp
from jax import lax
from jax.experimental import pallas as pl
from jax.experimental.pallas import tpu as pltpu
from jax.sharding import PartitionSpec as P

ITERS = 3
STEP = 0.2
SMOOTH = 2.0
PENALTY = 0.1
THRESHOLD = 0.2 * 0.25
KP = 160
CHUNKS = (160,)
BS = 128
UNROLL = 8
AHEAD = 4
RING = 6
F32 = jnp.float32
BF16 = jnp.bfloat16
SM = pl.BlockSpec(memory_space=pltpu.SMEM)
HBM = pl.BlockSpec(memory_space=pltpu.HBM)


def params(mib=56):
    return pltpu.CompilerParams(vmem_limit_bytes=mib << 20)


def cost(flops, moved):
    return pl.CostEstimate(flops=int(flops), bytes_accessed=int(moved), transcendentals=0)


def shape(dims, kind):
    return jax.ShapeDtypeStruct(dims, kind)


def shrink(x):
    return x - jnp.clip(x, -THRESHOLD, THRESHOLD)


def partial_fit(signal, weights, parts):
    dirs, wide = signal.shape
    rows = weights.shape[0]
    span = wide // parts

    def body(signal_ref, weights_ref, out_ref):
        out_ref[0] = jnp.dot(weights_ref[...], signal_ref[...], preferred_element_type=F32)

    return pl.pallas_call(
        body,
        grid=(parts,),
        in_specs=[
            pl.BlockSpec((dirs, span), lambda i: (0, i)),
            pl.BlockSpec((rows, dirs), lambda i: (0, 0)),
        ],
        out_specs=pl.BlockSpec((1, rows, span), lambda i: (i, 0, 0)),
        out_shape=shape((parts, rows, span), F32),
        compiler_params=params(),
        cost_estimate=cost(2 * rows * dirs * wide, 2 * dirs * wide + 4 * rows * wide),
        name="partial_fit",
    )(signal, weights)


def plan_tasks(count, index):
    rows, slots = index.shape
    room = rows * ((slots + 1) // 2 + 1) + UNROLL

    def body(count_ref, index_ref, own_ref, far_ref, steps_ref):
        def row(r, carry):
            n_own, n_far = carry

            def put(ref, n, held, m, c, zero):
                first = r + 32 * m + 1024 * m + 32768 * c + 4194304 * zero
                whole = held + 1024 * (m - ((held // 32) % 32)) + 4194304 * (c - zero)
                fresh = held < 0
                at = jnp.where(fresh, n, n - 1)
                ref[at] = jnp.where(fresh, first, whole)
                return jnp.where(fresh, n + 1, n), jnp.where(fresh, first, -1)

            def slot(m, inner):
                n_own, n_far, h_own, h_far = inner
                c = index_ref[r, m]
                near = c < rows

                def yes():
                    n, h = put(own_ref, n_own, h_own, m, c, rows)
                    return n, n_far, h, h_far

                def no():
                    n, h = put(far_ref, n_far, h_far, m, c - rows, 48)
                    return n_own, n, h_own, h

                return lax.cond(near, yes, no)

            none = jnp.int32(-1)
            n_own, n_far, _, _ = lax.fori_loop(
                0, count_ref[r], slot, (n_own, n_far, none, none)
            )
            return n_own, n_far

        zero = jnp.int32(0)
        n_own, n_far = lax.fori_loop(0, rows, row, (zero, zero))
        for i in range(UNROLL):
            own_ref[n_own + i] = rows + 32768 * rows + 4194304 * rows
            far_ref[n_far + i] = rows + 32768 * 48 + 4194304 * 48
        steps_ref[0] = (n_own + UNROLL - 1) // UNROLL
        steps_ref[1] = (n_far + UNROLL - 1) // UNROLL

    return pl.pallas_call(
        body,
        in_specs=[SM, SM],
        out_specs=[SM, SM, SM],
        out_shape=[shape((room,), jnp.int32), shape((room,), jnp.int32), shape((2,), jnp.int32)],
        compiler_params=params(),
        cost_estimate=cost(1, 10_000_000),
        name="plan_tasks",
    )(count, index)


def send_blocks(want_ref, own, send_ref, sem):
    peers, cap = want_ref.shape
    for p in range(peers):
        for q in range(cap):
            pltpu.make_async_copy(own.at[want_ref[p, q]], send_ref.at[p * cap + q], sem).start()


def wait_all(ref, sem):
    pltpu.make_async_copy(ref, ref, sem).wait()


def first_pack(initial, want):
    rows, wide = initial.shape
    blocks = wide // BS
    peers, cap = want.shape

    def body(want_ref, initial_ref, own_ref, send_ref, held, own, sems):
        load = pltpu.make_async_copy(initial_ref, held, sems.at[0])
        load.start()
        load.wait()
        for r in range(blocks):
            block = held[:, r * BS : (r + 1) * BS]
            block = jnp.concatenate([block, jnp.ones((KP - rows, BS), F32)], axis=0)
            own[r] = block.astype(BF16)
        send_blocks(want_ref, own, send_ref, sems.at[1])
        keep = pltpu.make_async_copy(own, own_ref, sems.at[2])
        keep.start()
        wait_all(send_ref, sems.at[1])
        keep.wait()

    return pl.pallas_call(
        body,
        in_specs=[SM, HBM],
        out_specs=[HBM, HBM],
        out_shape=[shape((blocks, KP, BS), BF16), shape((peers * cap, KP, BS), BF16)],
        scratch_shapes=[
            pltpu.VMEM((rows, wide), F32),
            pltpu.VMEM((blocks, KP, BS), BF16),
            pltpu.SemaphoreType.DMA((3,)),
        ],
        compiler_params=params(),
        cost_estimate=cost(1, 4 * rows * wide + 2 * (blocks + peers * cap) * KP * BS),
        name="first_pack",
    )(want, initial)


def local_terms(pieces, gram, sphere, sphere_t):
    wide = pieces[0].shape[1]
    rows = sum(p.shape[0] for p in pieces)
    ns = sphere.shape[0]
    tile = 512

    def body(*refs):
        ins, (g_ref, s_ref, st_ref), outs = refs[: len(pieces)], refs[len(pieces) :][:3], refs[len(pieces) + 3 :]
        c = jnp.concatenate(
            [r[...] for r in ins] + ([jnp.zeros((KP - rows, tile), F32)] if rows < KP else []), axis=0
        )
        hi = c.astype(BF16)
        lo = (c - hi.astype(F32)).astype(BF16)
        g = g_ref[...]
        gh = g.astype(BF16)
        gl = (g - gh.astype(F32)).astype(BF16)
        fid = jnp.dot(gh, hi, preferred_element_type=F32)
        fid += jnp.dot(gh, lo, preferred_element_type=F32)
        fid += jnp.dot(gl, hi, preferred_element_type=F32)
        amplitude = jnp.dot(s_ref[...], hi, preferred_element_type=F32)
        negative = jnp.minimum(amplitude, 0.0).astype(BF16)
        pulled = jnp.dot(st_ref[...], negative, preferred_element_type=F32)
        value = c - STEP * (fid + SMOOTH * c + PENALTY * pulled)
        at = 0
        for ref, k in zip(outs, CHUNKS):
            ref[...] = value[at : at + k]
            at += k

    def whole(*dims):
        return pl.BlockSpec(dims, lambda i: (0,) * len(dims))

    return pl.pallas_call(
        body,
        grid=(wide // tile,),
        in_specs=[pl.BlockSpec((p.shape[0], tile), lambda i: (0, i)) for p in pieces]
        + [whole(KP, KP), whole(ns, KP), whole(KP, ns)],
        out_specs=[pl.BlockSpec((k, tile), lambda i: (0, i)) for k in CHUNKS],
        out_shape=[shape((k, wide), F32) for k in CHUNKS],
        compiler_params=params(),
        cost_estimate=cost(2 * wide * KP * (3 * KP + 2 * ns), 8 * KP * wide),
        name="local_terms",
    )(*pieces, gram, sphere, sphere_t)


def run_tasks(tasks_ref, steps, blocks_ref, sim_ref, acc_ref, ring, sems, before):
    rows = sim_ref.shape[0]
    nt = (((1,), (1,)), ((), ()))
    wide = 2 * UNROLL

    def fetch(s):
        slot = lax.rem(s, RING)
        for u in range(UNROLL):
            t = tasks_ref[s * UNROLL + u]
            r = jnp.minimum(t & 31, rows - 1)
            for i, m in enumerate(((t >> 5) & 31, (t >> 10) & 31)):
                to = ring.at[slot * wide + (2 * u + i)]
                pltpu.make_async_copy(sim_ref.at[r, m], to, sems.at[slot]).start()

    for s in range(AHEAD):

        @pl.when(s < steps)
        def _():
            fetch(jnp.int32(s))

    before()

    def step(s, carry):
        slot = lax.rem(s, RING)

        @pl.when(s + AHEAD < steps)
        def _():
            fetch(s + AHEAD)

        wait_all(ring.at[pl.ds(slot * wide, wide)], sems.at[slot])
        made = []
        for u in range(UNROLL):
            t = tasks_ref[s * UNROLL + u]
            at = slot * wide + 2 * u
            left = jnp.concatenate([blocks_ref[(t >> 15) & 127], blocks_ref[(t >> 22) & 127]], axis=1)
            right = jnp.concatenate([ring[at], ring[at + 1]], axis=1)
            made.append((t & 31, lax.dot_general(left, right, nt, preferred_element_type=F32)))
        for r, d in made:
            acc_ref[r] = acc_ref[r] + d
        return carry

    lax.fori_loop(0, steps, step, 0)


def graph_call(which, tasks, steps, blocks, similarity, extra, finish, out_shape, scratch, sems, name):
    rows = similarity.shape[0]
    given, k, _ = blocks.shape
    loaded = [x for x in extra if x.dtype != jnp.int32]

    def body(tasks_ref, steps_ref, blocks_ref, sim_ref, *rest):
        extra_refs, rest = rest[: len(extra)], rest[len(extra) :]
        outs, rest = rest[: len(out_shape)], rest[len(out_shape) :]
        held, acc, ring, ring_sems, load_sems, *rest = rest
        buffers, rest = rest[: len(loaded)], rest[len(loaded) :]
        own_scratch, own_sems = rest[: len(scratch)], rest[len(scratch) :]
        first = pltpu.make_async_copy(blocks_ref, held.at[pl.ds(0, given)], load_sems.at[0])
        first.start()
        held[given] = jnp.zeros((k, BS), BF16)
        for r in range(rows + 1):
            acc[r] = jnp.zeros((k, BS), F32)
        loads, ready = [], []
        left = list(buffers)
        for x, ref in zip(extra, extra_refs):
            if x.dtype == jnp.int32:
                ready.append(ref)
                continue
            to = left.pop(0)
            ready.append(to)
            loads.append(pltpu.make_async_copy(ref, to, load_sems.at[len(loads) + 1]))

        def before():
            for load in loads:
                load.start()
            first.wait()

        run_tasks(tasks_ref, steps_ref[which], held, sim_ref, acc, ring, ring_sems, before)
        for load in loads:
            load.wait()
        finish(acc, ready, outs, own_scratch, own_sems[0] if own_sems else None)

    return pl.pallas_call(
        body,
        in_specs=[SM, SM, HBM, HBM] + [SM if x.dtype == jnp.int32 else HBM for x in extra],
        out_specs=[HBM] * len(out_shape),
        out_shape=out_shape,
        scratch_shapes=[
            pltpu.VMEM((given + 1, k, BS), BF16),
            pltpu.VMEM((rows + 1, k, BS), F32),
            pltpu.VMEM((RING * 2 * UNROLL, BS, BS), BF16),
            pltpu.SemaphoreType.DMA((RING,)),
            pltpu.SemaphoreType.DMA((len(loaded) + 1,)),
        ]
        + [pltpu.VMEM(x.shape, x.dtype) for x in loaded]
        + scratch
        + [pltpu.SemaphoreType.DMA((sems,))],
        compiler_params=params(),
        cost_estimate=cost(2 * k * BS * BS * rows * 14, 8_000_000),
        name=name,
    )(tasks, steps, blocks, similarity, *extra)


def first_own(tasks, steps, own, similarity):
    rows = similarity.shape[0]
    k = own.shape[1]

    def finish(acc, extra, outs, scratch, sems):
        out = pltpu.make_async_copy(acc.at[pl.ds(0, rows)], outs[0], sems.at[0])
        out.start()
        out.wait()

    (summed,) = graph_call(
        0, tasks, steps, own, similarity, [], finish, [shape((rows, k, BS), F32)], [], 1, "first_own"
    )
    return summed


def first_far(tasks, steps, recv, similarity, summed, bases):
    rows = similarity.shape[0]
    wide = rows * BS

    def finish(acc, extra, outs, scratch, sems):
        sum_ref, *base_refs = extra
        for r in range(rows):
            at = slice(r * BS, (r + 1) * BS)
            total = acc[r] + sum_ref[r]
            factor = (STEP * SMOOTH) / total[KP - 1 : KP]
            total = total * factor
            low = 0
            for base_ref, to, k in zip(base_refs, scratch, CHUNKS):
                to[:, at] = base_ref[:, at] + total[low : low + k]
                low += k
            scratch[-1][:, at] = jnp.broadcast_to(factor, (8, BS))
        copies = [pltpu.make_async_copy(s, o, sems.at[i]) for i, (s, o) in enumerate(zip(scratch, outs))]
        for copy in copies:
            copy.start()
        for copy in copies:
            copy.wait()

    dims = [(k, wide) for k in CHUNKS] + [(8, wide)]
    *mixed, factor = graph_call(
        1,
        tasks,
        steps,
        recv,
        similarity,
        [summed, *bases],
        finish,
        [shape(d, F32) for d in dims],
        [pltpu.VMEM(d, F32) for d in dims],
        len(dims),
        "first_far",
    )
    return mixed, factor


def next_own(tasks, steps, own, similarity, base, fitted, factor):
    rows = similarity.shape[0]
    wide = rows * BS
    k = own.shape[1]

    def finish(acc, extra, outs, scratch, sems):
        base_ref, fit_ref, factor_ref = extra
        for r in range(rows):
            at = slice(r * BS, (r + 1) * BS)
            scratch[0][:, at] = base_ref[:, at] + STEP * fit_ref[:, at] + acc[r] * factor_ref[0:1, at]
        out = pltpu.make_async_copy(scratch[0], outs[0], sems.at[0])
        out.start()
        out.wait()

    (pre,) = graph_call(
        0,
        tasks,
        steps,
        own,
        similarity,
        [base, fitted, factor],
        finish,
        [shape((k, wide), F32)],
        [pltpu.VMEM((k, wide), F32)],
        1,
        "next_own",
    )
    return pre


def hand_on(values, want_ref, outs, scratch, sems):
    out_ref, own_ref, send_ref = outs
    out, own = scratch
    for r in range(own.shape[0]):
        value = values(r)
        out[:, r * BS : (r + 1) * BS] = value
        own[r] = value.astype(BF16)
    send_blocks(want_ref, own, send_ref, sems.at[0])
    copies = [
        pltpu.make_async_copy(own, own_ref, sems.at[1]),
        pltpu.make_async_copy(out, out_ref, sems.at[2]),
    ]
    for copy in copies:
        copy.start()
    wait_all(send_ref, sems.at[0])
    for copy in copies:
        copy.wait()


def next_far(tasks, steps, recv, similarity, pre, factor, want):
    rows = similarity.shape[0]
    wide = rows * BS
    k = recv.shape[1]

    def finish(acc, extra, outs, scratch, sems):
        pre_ref, factor_ref, want_ref = extra

        def values(r):
            at = slice(r * BS, (r + 1) * BS)
            return shrink(pre_ref[:, at] + acc[r] * factor_ref[0:1, at])

        hand_on(values, want_ref, outs, scratch, sems)

    return graph_call(
        1,
        tasks,
        steps,
        recv,
        similarity,
        [pre, factor, want],
        finish,
        [shape((k, wide), F32), shape((rows, k, BS), BF16), shape(recv.shape, BF16)],
        [pltpu.VMEM((k, wide), F32), pltpu.VMEM((rows, k, BS), BF16)],
        3,
        "next_far",
    )


def last_far(tasks, steps, recv, similarity, pre, factor, above, out_rows):
    rows = similarity.shape[0]
    wide = rows * BS

    def finish(acc, extra, outs, scratch, sems):
        pre_ref, factor_ref, *done = extra
        (out,) = scratch
        low = 0
        for ref in done:
            out[low : low + ref.shape[0], :] = ref[...]
            low += ref.shape[0]
        for r in range(rows):
            at = slice(r * BS, (r + 1) * BS)
            value = shrink(pre_ref[:, at] + acc[r] * factor_ref[0:1, at])
            out[low:out_rows, at] = value[: out_rows - low]
        copy = pltpu.make_async_copy(out, outs[0], sems.at[0])
        copy.start()
        copy.wait()

    (coeffs,) = graph_call(
        1,
        tasks,
        steps,
        recv,
        similarity,
        [pre, factor, *above],
        finish,
        [shape((out_rows, wide), F32)],
        [pltpu.VMEM((out_rows, wide), F32)],
        1,
        "last_far",
    )
    return coeffs


def finish_first(mixed, fitted, want):
    k, wide = mixed.shape
    rows = wide // BS
    peers, cap = want.shape

    def body(want_ref, mixed_ref, fit_ref, out_ref, own_ref, send_ref, mix, fit, out, own, sems):
        loads = [
            pltpu.make_async_copy(mixed_ref, mix, sems.at[3]),
            pltpu.make_async_copy(fit_ref, fit, sems.at[4]),
        ]
        for load in loads:
            load.start()
        for load in loads:
            load.wait()

        def values(r):
            at = slice(r * BS, (r + 1) * BS)
            return shrink(mix[:, at] + STEP * fit[:, at])

        hand_on(values, want_ref, (out_ref, own_ref, send_ref), (out, own), sems)

    return pl.pallas_call(
        body,
        in_specs=[SM, HBM, HBM],
        out_specs=[HBM] * 3,
        out_shape=[
            shape((k, wide), F32),
            shape((rows, k, BS), BF16),
            shape((peers * cap, k, BS), BF16),
        ],
        scratch_shapes=[
            pltpu.VMEM((k, wide), F32),
            pltpu.VMEM((k, wide), F32),
            pltpu.VMEM((k, wide), F32),
            pltpu.VMEM((rows, k, BS), BF16),
            pltpu.SemaphoreType.DMA((5,)),
        ],
        compiler_params=params(),
        cost_estimate=cost(1, 12 * k * wide),
        name="finish_first",
    )(want, mixed, fitted)


def local(
    signal,
    response,
    sphere_basis,
    initial,
    similarity,
    neighbour_count,
    neighbour_index,
    fetch_list,
):
    coef_count = initial.shape[0]
    peers = lax.axis_size("vox")
    parts = lax.axis_size("dir")
    dirs = signal.shape[0]
    pad = KP - coef_count

    response = jnp.pad(response, ((0, pad), (0, 0)))
    mine = lax.dynamic_slice_in_dim(response, lax.axis_index("dir") * dirs, dirs, axis=1)
    fitted = []
    low = 0
    for k in CHUNKS:
        piece = partial_fit(signal, mine[low : low + k], parts)
        low += k
        fitted.append(
            lax.psum_scatter(piece.reshape(parts * k, -1), "dir", scatter_dimension=0, tiled=True)
        )
    want = lax.all_to_all(
        fetch_list.reshape(peers, -1), "vox", split_axis=0, concat_axis=0, tiled=True
    )
    gram = lax.dot_general(response, response, (((1,), (1,)), ((), ())), preferred_element_type=F32)
    sphere = jnp.pad(sphere_basis, ((0, 0), (0, pad)))
    sphere_t = sphere.T

    def exchange(send):
        moved = lax.all_to_all(
            send.reshape(peers, -1, BS), "vox", split_axis=0, concat_axis=0, tiled=True
        )
        return moved.reshape(send.shape)

    near, far, steps = plan_tasks(neighbour_count, neighbour_index)

    own, send = first_pack(initial, want)
    recv = exchange(send)
    base = local_terms([initial], gram, sphere, sphere_t)
    summed = first_own(near, steps, own, similarity)
    mixed, factor = first_far(far, steps, recv, similarity, summed, base)
    state = [finish_first(m, f, want) for m, f in zip(mixed, fitted)]
    for iteration in range(1, ITERS):
        recv = [exchange(send) for _, _, send in state]
        base = local_terms([c for c, _, _ in state], gram, sphere, sphere_t)
        pre = [
            next_own(near, steps, own, similarity, b, f, factor)
            for (_, own, _), b, f in zip(state, base, fitted)
        ]
        if iteration < ITERS - 1:
            state = [
                next_far(far, steps, v, similarity, p, factor, want) for v, p in zip(recv, pre)
            ]
        else:
            above = [
                next_far(far, steps, v, similarity, p, factor, want)[0]
                for v, p in zip(recv[:-1], pre[:-1])
            ]
            coeffs = last_far(far, steps, recv[-1], similarity, pre[-1], factor, above, coef_count)
    return coeffs


def solution(mesh):
    in_specs = (
        P("dir", "vox"),
        P(),
        P(),
        P(None, ("vox", "dir")),
        P(("vox", "dir"), None, None, None),
        P(("vox", "dir")),
        P(("vox", "dir"), None),
        P(("vox", "dir"), None, None),
    )
    out_specs = P(None, ("vox", "dir"))
    return jax.shard_map(local, mesh=mesh, in_specs=in_specs, out_specs=out_specs, check_vma=False)
```

```python
import jax
import jax.numpy as jnp
from jax import lax
from jax.experimental import pallas as pl
from jax.experimental.pallas import tpu as pltpu
from jax.sharding import PartitionSpec as P

ITERS = 3
STEP = 0.2
SMOOTH = 2.0
PENALTY = 0.1
THRESHOLD = 0.2 * 0.25
KP = 160
CHUNKS = (160,)
BS = 128
UNROLL = 8
AHEAD = 4
RING = 6
F32 = jnp.float32
BF16 = jnp.bfloat16
SM = pl.BlockSpec(memory_space=pltpu.SMEM)
HBM = pl.BlockSpec(memory_space=pltpu.HBM)
VM = pl.BlockSpec(memory_space=pltpu.VMEM)
ANY = pl.BlockSpec(memory_space=pl.ANY)


def params(mib=52):
    return pltpu.CompilerParams(vmem_limit_bytes=mib << 20)


def cost(flops, moved):
    return pl.CostEstimate(flops=int(flops), bytes_accessed=int(moved), transcendentals=0)


def shape(dims, kind):
    return jax.ShapeDtypeStruct(dims, kind)


def shrink(x):
    return x - jnp.clip(x, -THRESHOLD, THRESHOLD)


def partial_fit(place, signal, response, parts):
    dirs, wide = signal.shape
    rows = response.shape[0]
    span = wide // parts
    blocks = span // BS

    def body(place_ref, signal_ref, given_ref, out_ref, held, response_ref, weights, out, sems):
        whole = pltpu.make_async_copy(given_ref, response_ref, sems.at[2 * parts])
        whole.start()
        def load(i):
            return pltpu.make_async_copy(signal_ref.at[:, pl.ds(i * span, span)], held.at[i], sems.at[i])

        def store(i):
            return pltpu.make_async_copy(out.at[i], out_ref.at[i], sems.at[parts + i])

        for i in range(parts):
            load(i).start()
        whole.wait()
        for i in range(parts):

            @pl.when(place_ref[0] == i)
            def _():
                weights[...] = response_ref[:, i * dirs : (i + 1) * dirs]

        for i in range(parts):
            load(i).wait()
            value = jnp.dot(weights[...], held[i], preferred_element_type=F32)
            for b in range(blocks):
                out[i, pl.ds(b, rows, stride=blocks), :] = value[:, b * BS : (b + 1) * BS]
            store(i).start()
        for i in range(parts):
            store(i).wait()

    return pl.pallas_call(
        body,
        in_specs=[SM, HBM, HBM],
        out_specs=HBM,
        out_shape=shape((parts, rows * blocks, BS), F32),
        scratch_shapes=[
            pltpu.VMEM((parts, dirs, span), BF16),
            pltpu.VMEM(response.shape, BF16),
            pltpu.VMEM((rows, dirs), BF16),
            pltpu.VMEM((parts, rows * blocks, BS), F32),
            pltpu.SemaphoreType.DMA((2 * parts + 1,)),
        ],
        compiler_params=params(),
        cost_estimate=cost(2 * rows * dirs * wide, 2 * dirs * wide + 4 * rows * wide),
        name="partial_fit",
    )(place, signal, response)


def set_up(count, index, response, sphere_t, fetched):
    rows, slots = index.shape
    coefs, ns = sphere_t.shape
    room = rows * (slots + 1) + 2 * UNROLL

    def body(count_ref, index_ref, response_ref, sphere_ref, list_ref, steps_ref, g_ref, s_ref, st_ref):
        def row(r, carry):
            def slot(m, inner):
                n_own, n_far = inner
                c = index_ref[r, m]
                near = c < rows
                at = jnp.where(near, n_own, n_far + room)
                list_ref[at] = r + 32 * m + 1024 * jnp.where(near, c, c - rows)
                one = jnp.where(near, 1, 0)
                return n_own + one, n_far + (1 - one)

            n_own, n_far = lax.fori_loop(0, count_ref[r], slot, carry)
            list_ref[n_own] = r + 1024 * rows
            list_ref[n_far + room] = r + 1024 * fetched
            return n_own + (n_own & 1), n_far + (n_far & 1)

        zero = jnp.int32(0)
        n_own, n_far = lax.fori_loop(0, rows, row, (zero, zero))
        for i in range(2 * UNROLL):
            list_ref[n_own + i] = rows + 1024 * rows
            list_ref[n_far + room + i] = rows + 1024 * fetched
        step = 2 * UNROLL
        steps_ref[0] = (n_own + step - 1) // step
        steps_ref[1] = (n_far + step - 1) // step

        def taller(x):
            x = x.astype(F32)
            return jnp.concatenate([x, jnp.zeros((KP - coefs, x.shape[1]), F32)], axis=0)

        low = taller(response_ref[...]).astype(BF16)
        nt = (((1,), (1,)), ((), ()))
        g_ref[...] = lax.dot_general(low, low, nt, preferred_element_type=F32)
        sphere = taller(sphere_ref[...])
        st_ref[...] = sphere.astype(BF16)
        s_ref[...] = sphere.T.astype(BF16)

    return pl.pallas_call(
        body,
        in_specs=[SM, SM, VM, VM],
        out_specs=[SM, SM, VM, VM, VM],
        out_shape=[
            shape((2 * room,), jnp.int32),
            shape((2,), jnp.int32),
            shape((KP, KP), F32),
            shape((ns, KP), BF16),
            shape((KP, ns), BF16),
        ],
        compiler_params=params(),
        cost_estimate=cost(1, 16_000_000),
        name="set_up",
    )(count, index, response, sphere_t)


def send_blocks(want_ref, own, send_ref, sem):
    peers, cap = want_ref.shape
    for p in range(peers):
        for q in range(cap):
            pltpu.make_async_copy(own.at[want_ref[p, q]], send_ref.at[p * cap + q], sem).start()


def wait_all(ref, sem):
    pltpu.make_async_copy(ref, ref, sem).wait()


def first_pack(initial, want):
    rows, wide = initial.shape
    blocks = wide // BS
    peers, cap = want.shape

    def body(want_ref, initial_ref, own_ref, send_ref, order_ref, ends_ref, held, own, sems):
        load = pltpu.make_async_copy(initial_ref, held, sems.at[0])
        load.start()
        load.wait()
        for r in range(blocks):
            block = held[:, r * BS : (r + 1) * BS]
            block = jnp.concatenate([block, jnp.ones((KP - rows, BS), F32)], axis=0)
            own[r] = block.astype(BF16)
        send_blocks(want_ref, own, send_ref, sems.at[1])
        keep = pltpu.make_async_copy(own, own_ref, sems.at[2])
        keep.start()
        for r in range(blocks):
            ends_ref[r] = 0
        for p in range(peers):
            for q in range(cap):
                w = want_ref[p, q]
                ends_ref[w] = ends_ref[w] + 1
        before = jnp.int32(0)
        for r in range(blocks):
            here = ends_ref[r]
            ends_ref[r] = before
            before = before + here
        for p in range(peers):
            for q in range(cap):
                w = want_ref[p, q]
                at = ends_ref[w]
                order_ref[at] = p * cap + q
                ends_ref[w] = at + 1
        wait_all(send_ref, sems.at[1])
        keep.wait()

    return pl.pallas_call(
        body,
        in_specs=[SM, HBM],
        out_specs=[HBM, HBM, SM, SM],
        out_shape=[
            shape((blocks, KP, BS), BF16),
            shape((peers * cap, KP, BS), BF16),
            shape((peers * cap,), jnp.int32),
            shape((blocks,), jnp.int32),
        ],
        scratch_shapes=[
            pltpu.VMEM((rows, wide), F32),
            pltpu.VMEM((blocks, KP, BS), BF16),
            pltpu.SemaphoreType.DMA((3,)),
        ],
        compiler_params=params(),
        cost_estimate=cost(1, 4 * rows * wide + 2 * (blocks + peers * cap) * KP * BS),
        name="first_pack",
    )(want, initial)


def local_terms(pieces, gram, sphere, sphere_t):
    wide = pieces[0].shape[1]
    rows = sum(p.shape[0] for p in pieces)
    ns = sphere.shape[0]
    tile = 512

    def body(*refs):
        ins, (g_ref, s_ref, st_ref), outs = refs[: len(pieces)], refs[len(pieces) :][:3], refs[len(pieces) + 3 :]
        c = jnp.concatenate(
            [r[...] for r in ins] + ([jnp.zeros((KP - rows, tile), F32)] if rows < KP else []), axis=0
        )
        hi = c.astype(BF16)
        lo = (c - hi.astype(F32)).astype(BF16)
        g = g_ref[...]
        gh = g.astype(BF16)
        gl = (g - gh.astype(F32)).astype(BF16)
        fid = jnp.dot(gh, hi, preferred_element_type=F32)
        fid += jnp.dot(gh, lo, preferred_element_type=F32)
        fid += jnp.dot(gl, hi, preferred_element_type=F32)
        amplitude = jnp.dot(s_ref[...], hi, preferred_element_type=F32)
        negative = jnp.minimum(amplitude, 0.0).astype(BF16)
        pulled = jnp.dot(st_ref[...], negative, preferred_element_type=F32)
        value = c - STEP * (fid + SMOOTH * c + PENALTY * pulled)
        at = 0
        for ref, k in zip(outs, CHUNKS):
            ref[...] = value[at : at + k]
            at += k

    def whole(*dims):
        return pl.BlockSpec(dims, lambda i: (0,) * len(dims))

    return pl.pallas_call(
        body,
        grid=(wide // tile,),
        in_specs=[pl.BlockSpec((p.shape[0], tile), lambda i: (0, i)) for p in pieces]
        + [whole(KP, KP), whole(ns, KP), whole(KP, ns)],
        out_specs=[pl.BlockSpec((k, tile), lambda i: (0, i)) for k in CHUNKS],
        out_shape=[shape((k, wide), F32) for k in CHUNKS],
        compiler_params=params(),
        cost_estimate=cost(2 * wide * KP * (3 * KP + 2 * ns), 8 * KP * wide),
        name="local_terms",
    )(*pieces, gram, sphere, sphere_t)


def run_tasks(list_ref, start, steps, blocks_ref, sim_ref, acc_ref, ring, sems, before, loaded, finish_row):
    rows = sim_ref.shape[0]
    nt = (((1,), (1,)), ((), ()))
    wide = 2 * UNROLL

    def fetch(s):
        slot = lax.rem(s, RING)
        for u in range(wide):
            e = list_ref[start + s * wide + u]
            r = jnp.minimum(e & 31, rows - 1)
            to = ring.at[slot * wide + u]
            pltpu.make_async_copy(sim_ref.at[r, (e >> 5) & 31], to, sems.at[slot]).start()

    for s in range(AHEAD):

        @pl.when(s < steps)
        def _():
            fetch(jnp.int32(s))

    before()

    def step(s, done):
        slot = lax.rem(s, RING)

        @pl.when(s + AHEAD < steps)
        def _():
            fetch(s + AHEAD)

        wait_all(ring.at[pl.ds(slot * wide, wide)], sems.at[slot])
        made = []
        for u in range(0, wide, 2):
            e, f = list_ref[start + s * wide + u], list_ref[start + s * wide + u + 1]
            at = slot * wide + u
            left = jnp.concatenate([blocks_ref[e >> 10], blocks_ref[f >> 10]], axis=1)
            right = jnp.concatenate([ring[at], ring[at + 1]], axis=1)
            made.append((e & 31, lax.dot_general(left, right, nt, preferred_element_type=F32)))
        for r, d in made:
            acc_ref[r] = acc_ref[r] + d
        if finish_row is None:
            return done
        pl.when(s == 0)(loaded)
        complete = list_ref[start + (s + 1) * wide] & 31
        lax.fori_loop(done, complete, lambda r, c: finish_row(r), None)
        return complete

    done = lax.fori_loop(0, steps, step, jnp.int32(0))
    if finish_row is None:
        loaded()
        return
    pl.when(steps == 0)(loaded)
    lax.fori_loop(done, rows, lambda r, c: finish_row(r), None)


def graph_call(
    which, tasks, steps, blocks, similarity, extra, finish, out_shape, scratch, sems, name, each_row=None
):
    rows = similarity.shape[0]
    given, k, _ = blocks.shape
    loaded = [x for x in extra if x.dtype != jnp.int32]

    def body(tasks_ref, steps_ref, blocks_ref, sim_ref, *rest):
        extra_refs, rest = rest[: len(extra)], rest[len(extra) :]
        outs, rest = rest[: len(out_shape)], rest[len(out_shape) :]
        held, acc, ring, ring_sems, load_sems, *rest = rest
        buffers, rest = rest[: len(loaded)], rest[len(loaded) :]
        own_scratch, own_sems = rest[: len(scratch)], rest[len(scratch) :]
        first = pltpu.make_async_copy(blocks_ref, held.at[pl.ds(0, given)], load_sems.at[0])
        first.start()
        held[given] = jnp.zeros((k, BS), BF16)
        for r in range(rows + 1):
            acc[r] = jnp.zeros((k, BS), F32)
        loads, ready = [], []
        left = list(buffers)
        for x, ref in zip(extra, extra_refs):
            if x.dtype == jnp.int32:
                ready.append(ref)
                continue
            to = left.pop(0)
            ready.append(to)
            loads.append(pltpu.make_async_copy(ref, to, load_sems.at[len(loads) + 1]))

        def before():
            for load in loads:
                load.start()
            first.wait()

        def all_loaded():
            for load in loads:
                load.wait()

        given_on = (acc, ready, outs, own_scratch, own_sems[0])
        finish_row = None if each_row is None else lambda r: each_row(r, *given_on)
        start = which * (tasks.shape[0] // 2)
        run_tasks(
            tasks_ref, start, steps_ref[which], held, sim_ref, acc, ring, ring_sems, before, all_loaded, finish_row
        )
        finish(*given_on)

    return pl.pallas_call(
        body,
        in_specs=[SM, SM, ANY, HBM] + [SM if x.dtype == jnp.int32 else HBM for x in extra],
        out_specs=[HBM] * len(out_shape),
        out_shape=out_shape,
        scratch_shapes=[
            pltpu.VMEM((given + 1, k, BS), BF16),
            pltpu.VMEM((rows + 1, k, BS), F32),
            pltpu.VMEM((RING * 2 * UNROLL, BS, BS), BF16),
            pltpu.SemaphoreType.DMA((RING,)),
            pltpu.SemaphoreType.DMA((len(loaded) + 1,)),
        ]
        + [pltpu.VMEM(x.shape, x.dtype) for x in loaded]
        + scratch
        + [pltpu.SemaphoreType.DMA((sems,))],
        compiler_params=params(),
        cost_estimate=cost(2 * k * BS * BS * rows * 14, 8_000_000),
        name=name,
    )(tasks, steps, blocks, similarity, *extra)


def first_own(tasks, steps, own, similarity):
    rows = similarity.shape[0]
    k = own.shape[1]

    def finish(acc, extra, outs, scratch, sems):
        out = pltpu.make_async_copy(acc.at[pl.ds(0, rows)], outs[0], sems.at[0])
        out.start()
        out.wait()

    (summed,) = graph_call(
        0, tasks, steps, own, similarity, [], finish, [shape((rows, k, BS), F32)], [], 1, "first_own"
    )
    return summed


def first_far(tasks, steps, recv, similarity, summed, bases):
    rows = similarity.shape[0]
    wide = rows * BS

    def finish(acc, extra, outs, scratch, sems):
        sum_ref, *base_refs = extra
        for r in range(rows):
            at = slice(r * BS, (r + 1) * BS)
            total = acc[r] + sum_ref[r]
            factor = (STEP * SMOOTH) / total[KP - 1 : KP]
            total = total * factor
            low = 0
            for base_ref, to, k in zip(base_refs, scratch, CHUNKS):
                to[:, at] = base_ref[:, at] + total[low : low + k]
                low += k
            scratch[-1][:, at] = jnp.broadcast_to(factor, (8, BS))
        copies = [pltpu.make_async_copy(s, o, sems.at[i]) for i, (s, o) in enumerate(zip(scratch, outs))]
        for copy in copies:
            copy.start()
        for copy in copies:
            copy.wait()

    dims = [(k, wide) for k in CHUNKS] + [(8, wide)]
    *mixed, factor = graph_call(
        1,
        tasks,
        steps,
        recv,
        similarity,
        [summed, *bases],
        finish,
        [shape(d, F32) for d in dims],
        [pltpu.VMEM(d, F32) for d in dims],
        len(dims),
        "first_far",
    )
    return mixed, factor


def next_own(tasks, steps, own, similarity, base, flat, factor):
    rows = similarity.shape[0]
    wide = rows * BS
    k = own.shape[1]

    def finish(acc, extra, outs, scratch, sems):
        base_ref, flat_ref, factor_ref = extra
        real = flat_ref.shape[0] // rows
        for r in range(rows):
            at = slice(r * BS, (r + 1) * BS)
            part = flat_ref[pl.ds(r, real, stride=rows), :]
            part = jnp.concatenate([part, jnp.zeros((k - real, BS), F32)], axis=0)
            scratch[0][:, at] = base_ref[:, at] + STEP * part + acc[r] * factor_ref[0:1, at]
        out = pltpu.make_async_copy(scratch[0], outs[0], sems.at[0])
        out.start()
        out.wait()

    (pre,) = graph_call(
        0,
        tasks,
        steps,
        own,
        similarity,
        [base, flat, factor],
        finish,
        [shape((k, wide), F32)],
        [pltpu.VMEM((k, wide), F32)],
        1,
        "next_own",
    )
    return pre


def hand_on(r, value, order_ref, ends_ref, outs, scratch, sems):
    out_ref, own_ref, send_ref = outs
    out, own = scratch
    out[r] = value
    own[r] = value.astype(BF16)
    at = pl.ds(pl.multiple_of(r * BS, BS), BS)

    def send(j, carry):
        pltpu.make_async_copy(own.at[r], send_ref.at[order_ref[j]], sems.at[0]).start()
        return carry

    lax.fori_loop(jnp.where(r == 0, 0, ends_ref[jnp.maximum(r - 1, 0)]), ends_ref[r], send, 0)
    pltpu.make_async_copy(own.at[r], own_ref.at[r], sems.at[1]).start()
    pltpu.make_async_copy(out.at[r], out_ref.at[:, at], sems.at[2]).start()


def handed(outs, sems):
    out_ref, own_ref, send_ref = outs
    wait_all(send_ref, sems.at[0])
    wait_all(own_ref, sems.at[1])
    wait_all(out_ref, sems.at[2])


def next_far(tasks, steps, recv, similarity, pre, factor, order, ends):
    rows = similarity.shape[0]
    wide = rows * BS
    k = recv.shape[1]

    def each_row(r, acc, extra, outs, scratch, sems):
        pre_ref, factor_ref, order_ref, ends_ref = extra
        at = pl.ds(pl.multiple_of(r * BS, BS), BS)
        value = shrink(pre_ref[:, at] + acc[r] * factor_ref[0:1, at])
        hand_on(r, value, order_ref, ends_ref, outs, scratch, sems)

    def finish(acc, extra, outs, scratch, sems):
        handed(outs, sems)

    return graph_call(
        1,
        tasks,
        steps,
        recv,
        similarity,
        [pre, factor, order, ends],
        finish,
        [shape((k, wide), F32), shape((rows, k, BS), BF16), shape(recv.shape, BF16)],
        [pltpu.VMEM((rows, k, BS), F32), pltpu.VMEM((rows, k, BS), BF16)],
        3,
        "next_far",
        each_row,
    )


def last_far(tasks, steps, recv, similarity, pre, factor, out_rows):
    rows = similarity.shape[0]
    wide = rows * BS

    def each_row(r, acc, extra, outs, scratch, sems):
        pre_ref, factor_ref = extra
        (out,) = scratch
        at = pl.ds(pl.multiple_of(r * BS, BS), BS)
        value = shrink(pre_ref[:, at] + acc[r] * factor_ref[0:1, at])
        out[r] = value[:out_rows]
        pltpu.make_async_copy(out.at[r], outs[0].at[:, at], sems.at[r]).start()

    def finish(acc, extra, outs, scratch, sems):
        for r in range(rows):
            at = slice(r * BS, (r + 1) * BS)
            pltpu.make_async_copy(scratch[0].at[r], outs[0].at[:, at], sems.at[r]).wait()

    (coeffs,) = graph_call(
        1,
        tasks,
        steps,
        recv,
        similarity,
        [pre, factor],
        finish,
        [shape((out_rows, wide), F32)],
        [pltpu.VMEM((rows, out_rows, BS), F32)],
        rows,
        "last_far",
        each_row,
    )
    return coeffs


def finish_first(mixed, flat, order, ends):
    k, wide = mixed.shape
    blocks = wide // BS
    rows = flat.shape[0] // blocks
    fetched = order.shape[0]

    def body(order_ref, ends_ref, mixed_ref, flat_ref, out_ref, own_ref, send_ref, mix, held, out, own, sems):
        loads = [
            pltpu.make_async_copy(mixed_ref, mix, sems.at[3]),
            pltpu.make_async_copy(flat_ref, held, sems.at[4]),
        ]
        for load in loads:
            load.start()
        for load in loads:
            load.wait()
        outs = (out_ref, own_ref, send_ref)

        def each(r, carry):
            at = pl.ds(pl.multiple_of(r * BS, BS), BS)
            part = held[pl.ds(r, rows, stride=blocks), :]
            part = jnp.concatenate([part, jnp.zeros((k - rows, BS), F32)], axis=0)
            value = shrink(mix[:, at] + STEP * part)
            hand_on(r, value, order_ref, ends_ref, outs, (out, own), sems)
            return carry

        lax.fori_loop(0, blocks, each, 0)
        handed(outs, sems)

    return pl.pallas_call(
        body,
        in_specs=[SM, SM, HBM, HBM],
        out_specs=[HBM] * 3,
        out_shape=[
            shape((k, wide), F32),
            shape((blocks, k, BS), BF16),
            shape((fetched, k, BS), BF16),
        ],
        scratch_shapes=[
            pltpu.VMEM((k, wide), F32),
            pltpu.VMEM((rows * blocks, BS), F32),
            pltpu.VMEM((blocks, k, BS), F32),
            pltpu.VMEM((blocks, k, BS), BF16),
            pltpu.SemaphoreType.DMA((5,)),
        ],
        compiler_params=params(),
        cost_estimate=cost(1, 12 * k * wide),
        name="finish_first",
    )(order, ends, mixed, flat)


def local(
    signal,
    response,
    sphere_basis,
    initial,
    similarity,
    neighbour_count,
    neighbour_index,
    fetch_list,
):
    coef_count = initial.shape[0]
    peers = lax.axis_size("vox")
    parts = lax.axis_size("dir")
    dirs = signal.shape[0]

    place = lax.axis_index("dir").reshape(1).astype(jnp.int32)
    partial = partial_fit(place, signal, response, parts)
    flat = lax.psum_scatter(
        partial.reshape(-1, BS), "dir", scatter_dimension=0, tiled=True
    )
    lists, steps, gram, sphere, sphere_t = set_up(
        neighbour_count, neighbour_index, response, sphere_basis.T, fetch_list.size
    )
    want = lax.all_to_all(
        fetch_list.reshape(peers, -1), "vox", split_axis=0, concat_axis=0, tiled=True
    )
    def exchange(send):
        moved = lax.all_to_all(
            send.reshape(peers, -1, BS), "vox", split_axis=0, concat_axis=0, tiled=True
        )
        return moved.reshape(send.shape)

    own, send, order, ends = first_pack(initial, want)
    recv = exchange(send)
    (base,) = local_terms([initial], gram, sphere, sphere_t)
    summed = first_own(lists, steps, own, similarity)
    (mixed,), factor = first_far(lists, steps, recv, similarity, summed, [base])
    coeffs, own, send = finish_first(mixed, flat, order, ends)
    for iteration in range(1, ITERS):
        recv = exchange(send)
        (base,) = local_terms([coeffs], gram, sphere, sphere_t)
        pre = next_own(lists, steps, own, similarity, base, flat, factor)
        if iteration < ITERS - 1:
            coeffs, own, send = next_far(lists, steps, recv, similarity, pre, factor, order, ends)
        else:
            coeffs = last_far(lists, steps, recv, similarity, pre, factor, coef_count)
    return coeffs


def solution(mesh):
    in_specs = (
        P("dir", "vox"),
        P(),
        P(),
        P(None, ("vox", "dir")),
        P(("vox", "dir"), None, None, None),
        P(("vox", "dir")),
        P(("vox", "dir"), None),
        P(("vox", "dir"), None, None),
    )
    out_specs = P(None, ("vox", "dir"))
    return jax.shard_map(local, mesh=mesh, in_specs=in_specs, out_specs=out_specs, check_vma=False)
```

```python
import jax
import jax.numpy as jnp
from jax import lax
from jax.experimental import pallas as pl
from jax.experimental.pallas import tpu as pltpu
from jax.sharding import PartitionSpec as P

ITERS = 3
STEP = 0.2
SMOOTH = 2.0
PENALTY = 0.1
THRESHOLD = 0.2 * 0.25
KP = 160
CHUNKS = (160,)
BS = 128
UNROLL = 8
AHEAD = 4
RING = 6
F32 = jnp.float32
BF16 = jnp.bfloat16
SM = pl.BlockSpec(memory_space=pltpu.SMEM)
HBM = pl.BlockSpec(memory_space=pltpu.HBM)
VM = pl.BlockSpec(memory_space=pltpu.VMEM)
ANY = pl.BlockSpec(memory_space=pl.ANY)


def params(mib=52):
    return pltpu.CompilerParams(vmem_limit_bytes=mib << 20)


def cost(flops, moved):
    return pl.CostEstimate(flops=int(flops), bytes_accessed=int(moved), transcendentals=0)


def shape(dims, kind):
    return jax.ShapeDtypeStruct(dims, kind)


def shrink(x):
    return x - jnp.clip(x, -THRESHOLD, THRESHOLD)


def cut_signal(signal, targets, parts):
    dirs, wide = signal.shape
    span = wide // parts
    count = targets.shape[0]
    pairs = count // 2

    def body(targets_ref, signal_ref, *rest):
        outs, (held, sems) = rest[:pairs], rest[pairs:]

        def load(i):
            at = pl.multiple_of(targets_ref[i] * span, span)
            return pltpu.make_async_copy(signal_ref.at[:, pl.ds(at, span)], held.at[i], sems.at[i])

        def store(i):
            half = pl.ds(i % 2 * span, span)
            return pltpu.make_async_copy(held.at[i], outs[i // 2].at[:, half], sems.at[count + i])

        for i in range(count):
            load(i).start()
        for i in range(count):
            load(i).wait()
            store(i).start()
        for i in range(count):
            store(i).wait()

    return pl.pallas_call(
        body,
        in_specs=[SM, HBM],
        out_specs=[HBM] * pairs,
        out_shape=[shape((dirs, 2 * span), BF16)] * pairs,
        scratch_shapes=[
            pltpu.VMEM((count, dirs, span), BF16),
            pltpu.SemaphoreType.DMA((2 * count,)),
        ],
        compiler_params=params(),
        cost_estimate=cost(1, 4 * dirs * wide),
        name="cut_signal",
    )(targets, signal)


def fit_loads(halves, pieces, refs, buffers, sems):
    loads = []
    for i, (x, ref, to) in enumerate(zip(pieces, refs, buffers)):
        span = to.shape[1]
        loads.append(pltpu.make_async_copy(ref.at[:, pl.ds(halves[i] * span, span)], to, sems.at[i]))
    return loads


def add_fit(source_ref, weights, pieces, first, at):
    total = None
    for i, piece in enumerate(pieces):
        part = jnp.dot(weights[source_ref[first + i]], piece[:, at], preferred_element_type=F32)
        total = part if total is None else total + part
    return total


def early_fit(sources, weights, halves, pieces):
    parts, k, dirs = weights.shape
    span = pieces[0].shape[1] // 2
    count = len(pieces)
    tile = 512

    def body(source_ref, weights_ref, *refs):
        out_ref, *buffers = refs[count:]
        out, load_sems, sems = buffers[count:]
        buffers = buffers[:count]
        loads = fit_loads(halves, pieces, refs, buffers, load_sems)
        for load in loads:
            load.start()
        for load in loads:
            load.wait()
        for c in range(0, span, tile):
            at = slice(c, c + tile)
            out[:, at] = add_fit(source_ref, weights_ref, buffers, 0, at)
        keep = pltpu.make_async_copy(out, out_ref, sems.at[0])
        keep.start()
        keep.wait()

    return pl.pallas_call(
        body,
        in_specs=[SM, VM] + [HBM] * count,
        out_specs=HBM,
        out_shape=shape((k, span), F32),
        scratch_shapes=[pltpu.VMEM((dirs, span), BF16)] * count
        + [
            pltpu.VMEM((k, span), F32),
            pltpu.SemaphoreType.DMA((count,)),
            pltpu.SemaphoreType.DMA((1,)),
        ],
        compiler_params=params(),
        cost_estimate=cost(2 * k * dirs * count * span, 2 * dirs * count * span),
        name="early_fit",
    )(sources, weights, *pieces)


def set_up(count, index, response, sphere_t, parts, fetched):
    rows, slots = index.shape
    coefs, ns = sphere_t.shape
    dirs = response.shape[1] // parts
    room = rows * (slots + 1) + 2 * UNROLL

    def body(count_ref, index_ref, response_ref, sphere_ref, list_ref, steps_ref, w_ref, g_ref, s_ref, st_ref):
        def row(r, carry):
            def slot(m, inner):
                n_own, n_far = inner
                c = index_ref[r, m]
                near = c < rows
                at = jnp.where(near, n_own, n_far + room)
                list_ref[at] = r + 32 * m + 1024 * jnp.where(near, c, c - rows)
                one = jnp.where(near, 1, 0)
                return n_own + one, n_far + (1 - one)

            n_own, n_far = lax.fori_loop(0, count_ref[r], slot, carry)
            list_ref[n_own] = r + 1024 * rows
            list_ref[n_far + room] = r + 1024 * fetched
            return n_own + (n_own & 1), n_far + (n_far & 1)

        zero = jnp.int32(0)
        n_own, n_far = lax.fori_loop(0, rows, row, (zero, zero))
        for i in range(2 * UNROLL):
            list_ref[n_own + i] = rows + 1024 * rows
            list_ref[n_far + room + i] = rows + 1024 * fetched
        step = 2 * UNROLL
        steps_ref[0] = (n_own + step - 1) // step
        steps_ref[1] = (n_far + step - 1) // step

        def taller(x):
            x = x.astype(F32)
            return jnp.concatenate([x, jnp.zeros((KP - coefs, x.shape[1]), F32)], axis=0)

        tall = taller(response_ref[...])
        for i in range(parts):
            w_ref[i] = tall[:, i * dirs : (i + 1) * dirs].astype(BF16)
        low = tall.astype(BF16)
        nt = (((1,), (1,)), ((), ()))
        g_ref[...] = lax.dot_general(low, low, nt, preferred_element_type=F32)
        sphere = taller(sphere_ref[...])
        st_ref[...] = sphere.astype(BF16)
        s_ref[...] = sphere.T.astype(BF16)

    return pl.pallas_call(
        body,
        in_specs=[SM, SM, VM, VM],
        out_specs=[SM, SM, VM, VM, VM, VM],
        out_shape=[
            shape((2 * room,), jnp.int32),
            shape((2,), jnp.int32),
            shape((parts, KP, dirs), BF16),
            shape((KP, KP), F32),
            shape((ns, KP), BF16),
            shape((KP, ns), BF16),
        ],
        compiler_params=params(),
        cost_estimate=cost(1, 16_000_000),
        name="set_up",
    )(count, index, response, sphere_t)


def send_blocks(want_ref, own, send_ref, sem):
    peers, cap = want_ref.shape
    for p in range(peers):
        for q in range(cap):
            pltpu.make_async_copy(own.at[want_ref[p, q]], send_ref.at[p * cap + q], sem).start()


def wait_all(ref, sem):
    pltpu.make_async_copy(ref, ref, sem).wait()


def first_pack(initial, want):
    rows, wide = initial.shape
    blocks = wide // BS
    peers, cap = want.shape

    def body(want_ref, initial_ref, own_ref, send_ref, order_ref, ends_ref, held, own, sems):
        load = pltpu.make_async_copy(initial_ref, held, sems.at[0])
        load.start()
        load.wait()
        for r in range(blocks):
            block = held[:, r * BS : (r + 1) * BS]
            block = jnp.concatenate([block, jnp.ones((KP - rows, BS), F32)], axis=0)
            own[r] = block.astype(BF16)
        send_blocks(want_ref, own, send_ref, sems.at[1])
        keep = pltpu.make_async_copy(own, own_ref, sems.at[2])
        keep.start()
        for r in range(blocks):
            ends_ref[r] = 0
        for p in range(peers):
            for q in range(cap):
                w = want_ref[p, q]
                ends_ref[w] = ends_ref[w] + 1
        before = jnp.int32(0)
        for r in range(blocks):
            here = ends_ref[r]
            ends_ref[r] = before
            before = before + here
        for p in range(peers):
            for q in range(cap):
                w = want_ref[p, q]
                at = ends_ref[w]
                order_ref[at] = p * cap + q
                ends_ref[w] = at + 1
        wait_all(send_ref, sems.at[1])
        keep.wait()

    return pl.pallas_call(
        body,
        in_specs=[SM, HBM],
        out_specs=[HBM, HBM, SM, SM],
        out_shape=[
            shape((blocks, KP, BS), BF16),
            shape((peers * cap, KP, BS), BF16),
            shape((peers * cap,), jnp.int32),
            shape((blocks,), jnp.int32),
        ],
        scratch_shapes=[
            pltpu.VMEM((rows, wide), F32),
            pltpu.VMEM((blocks, KP, BS), BF16),
            pltpu.SemaphoreType.DMA((3,)),
        ],
        compiler_params=params(),
        cost_estimate=cost(1, 4 * rows * wide + 2 * (blocks + peers * cap) * KP * BS),
        name="first_pack",
    )(want, initial)


def local_terms(pieces, gram, sphere, sphere_t):
    wide = pieces[0].shape[1]
    rows = sum(p.shape[0] for p in pieces)
    ns = sphere.shape[0]
    tile = 512

    def body(*refs):
        ins, (g_ref, s_ref, st_ref), outs = refs[: len(pieces)], refs[len(pieces) :][:3], refs[len(pieces) + 3 :]
        c = jnp.concatenate(
            [r[...] for r in ins] + ([jnp.zeros((KP - rows, tile), F32)] if rows < KP else []), axis=0
        )
        hi = c.astype(BF16)
        lo = (c - hi.astype(F32)).astype(BF16)
        g = g_ref[...]
        gh = g.astype(BF16)
        gl = (g - gh.astype(F32)).astype(BF16)
        fid = jnp.dot(gh, hi, preferred_element_type=F32)
        fid += jnp.dot(gh, lo, preferred_element_type=F32)
        fid += jnp.dot(gl, hi, preferred_element_type=F32)
        amplitude = jnp.dot(s_ref[...], hi, preferred_element_type=F32)
        negative = jnp.minimum(amplitude, 0.0).astype(BF16)
        pulled = jnp.dot(st_ref[...], negative, preferred_element_type=F32)
        value = c - STEP * (fid + SMOOTH * c + PENALTY * pulled)
        at = 0
        for ref, k in zip(outs, CHUNKS):
            ref[...] = value[at : at + k]
            at += k

    def whole(*dims):
        return pl.BlockSpec(dims, lambda i: (0,) * len(dims))

    return pl.pallas_call(
        body,
        grid=(wide // tile,),
        in_specs=[pl.BlockSpec((p.shape[0], tile), lambda i: (0, i)) for p in pieces]
        + [whole(KP, KP), whole(ns, KP), whole(KP, ns)],
        out_specs=[pl.BlockSpec((k, tile), lambda i: (0, i)) for k in CHUNKS],
        out_shape=[shape((k, wide), F32) for k in CHUNKS],
        compiler_params=params(),
        cost_estimate=cost(2 * wide * KP * (3 * KP + 2 * ns), 8 * KP * wide),
        name="local_terms",
    )(*pieces, gram, sphere, sphere_t)


def run_tasks(list_ref, start, steps, blocks_ref, sim_ref, acc_ref, ring, sems, before, loaded, finish_row):
    rows = sim_ref.shape[0]
    nt = (((1,), (1,)), ((), ()))
    wide = 2 * UNROLL

    def fetch(s):
        slot = lax.rem(s, RING)
        for u in range(wide):
            e = list_ref[start + s * wide + u]
            r = jnp.minimum(e & 31, rows - 1)
            to = ring.at[slot * wide + u]
            pltpu.make_async_copy(sim_ref.at[r, (e >> 5) & 31], to, sems.at[slot]).start()

    for s in range(AHEAD):

        @pl.when(s < steps)
        def _():
            fetch(jnp.int32(s))

    before()

    def step(s, done):
        slot = lax.rem(s, RING)

        @pl.when(s + AHEAD < steps)
        def _():
            fetch(s + AHEAD)

        wait_all(ring.at[pl.ds(slot * wide, wide)], sems.at[slot])
        made = []
        for u in range(0, wide, 2):
            e, f = list_ref[start + s * wide + u], list_ref[start + s * wide + u + 1]
            at = slot * wide + u
            left = jnp.concatenate([blocks_ref[e >> 10], blocks_ref[f >> 10]], axis=1)
            right = jnp.concatenate([ring[at], ring[at + 1]], axis=1)
            made.append((e & 31, lax.dot_general(left, right, nt, preferred_element_type=F32)))
        for r, d in made:
            acc_ref[r] = acc_ref[r] + d
        if finish_row is None:
            return done
        pl.when(s == 0)(loaded)
        complete = list_ref[start + (s + 1) * wide] & 31
        lax.fori_loop(done, complete, lambda r, c: finish_row(r), None)
        return complete

    done = lax.fori_loop(0, steps, step, jnp.int32(0))
    if finish_row is None:
        loaded()
        return
    pl.when(steps == 0)(loaded)
    lax.fori_loop(done, rows, lambda r, c: finish_row(r), None)


def graph_call(
    which, tasks, steps, blocks, similarity, extra, finish, out_shape, scratch, sems, name, each_row=None
):
    rows = similarity.shape[0]
    given, k, _ = blocks.shape
    loaded = [x for x in extra if x.dtype != jnp.int32]

    def body(tasks_ref, steps_ref, blocks_ref, sim_ref, *rest):
        extra_refs, rest = rest[: len(extra)], rest[len(extra) :]
        outs, rest = rest[: len(out_shape)], rest[len(out_shape) :]
        held, acc, ring, ring_sems, load_sems, *rest = rest
        buffers, rest = rest[: len(loaded)], rest[len(loaded) :]
        own_scratch, own_sems = rest[: len(scratch)], rest[len(scratch) :]
        first = pltpu.make_async_copy(blocks_ref, held.at[pl.ds(0, given)], load_sems.at[0])
        first.start()
        held[given] = jnp.zeros((k, BS), BF16)
        for r in range(rows + 1):
            acc[r] = jnp.zeros((k, BS), F32)
        loads, ready = [], []
        left = list(buffers)
        for x, ref in zip(extra, extra_refs):
            if x.dtype == jnp.int32:
                ready.append(ref)
                continue
            to = left.pop(0)
            ready.append(to)
            loads.append(pltpu.make_async_copy(ref, to, load_sems.at[len(loads) + 1]))

        def before():
            for load in loads:
                load.start()
            first.wait()

        def all_loaded():
            for load in loads:
                load.wait()

        given_on = (acc, ready, outs, own_scratch, own_sems[0])
        finish_row = None if each_row is None else lambda r: each_row(r, *given_on)
        start = which * (tasks.shape[0] // 2)
        run_tasks(
            tasks_ref, start, steps_ref[which], held, sim_ref, acc, ring, ring_sems, before, all_loaded, finish_row
        )
        finish(*given_on)

    return pl.pallas_call(
        body,
        in_specs=[SM, SM, ANY, HBM] + [SM if x.dtype == jnp.int32 else HBM for x in extra],
        out_specs=[HBM] * len(out_shape),
        out_shape=out_shape,
        scratch_shapes=[
            pltpu.VMEM((given + 1, k, BS), BF16),
            pltpu.VMEM((rows + 1, k, BS), F32),
            pltpu.VMEM((RING * 2 * UNROLL, BS, BS), BF16),
            pltpu.SemaphoreType.DMA((RING,)),
            pltpu.SemaphoreType.DMA((len(loaded) + 1,)),
        ]
        + [pltpu.VMEM(x.shape, x.dtype) for x in loaded]
        + scratch
        + [pltpu.SemaphoreType.DMA((sems,))],
        compiler_params=params(),
        cost_estimate=cost(2 * k * BS * BS * rows * 14, 8_000_000),
        name=name,
    )(tasks, steps, blocks, similarity, *extra)


def first_own(tasks, steps, own, similarity):
    rows = similarity.shape[0]
    k = own.shape[1]

    def finish(acc, extra, outs, scratch, sems):
        out = pltpu.make_async_copy(acc.at[pl.ds(0, rows)], outs[0], sems.at[0])
        out.start()
        out.wait()

    (summed,) = graph_call(
        0, tasks, steps, own, similarity, [], finish, [shape((rows, k, BS), F32)], [], 1, "first_own"
    )
    return summed


def first_far(tasks, steps, recv, similarity, summed, bases):
    rows = similarity.shape[0]
    wide = rows * BS

    def finish(acc, extra, outs, scratch, sems):
        sum_ref, *base_refs = extra
        for r in range(rows):
            at = slice(r * BS, (r + 1) * BS)
            total = acc[r] + sum_ref[r]
            factor = (STEP * SMOOTH) / total[KP - 1 : KP]
            total = total * factor
            low = 0
            for base_ref, to, k in zip(base_refs, scratch, CHUNKS):
                to[:, at] = base_ref[:, at] + total[low : low + k]
                low += k
            scratch[-1][:, at] = jnp.broadcast_to(factor, (8, BS))
        copies = [pltpu.make_async_copy(s, o, sems.at[i]) for i, (s, o) in enumerate(zip(scratch, outs))]
        for copy in copies:
            copy.start()
        for copy in copies:
            copy.wait()

    dims = [(k, wide) for k in CHUNKS] + [(8, wide)]
    *mixed, factor = graph_call(
        1,
        tasks,
        steps,
        recv,
        similarity,
        [summed, *bases],
        finish,
        [shape(d, F32) for d in dims],
        [pltpu.VMEM(d, F32) for d in dims],
        len(dims),
        "first_far",
    )
    return mixed, factor


def next_own(tasks, steps, own, similarity, base, fit, factor):
    rows = similarity.shape[0]
    wide = rows * BS
    k = own.shape[1]

    def finish(acc, extra, outs, scratch, sems):
        base_ref, fit_ref, factor_ref = extra
        for r in range(rows):
            at = slice(r * BS, (r + 1) * BS)
            scratch[0][:, at] = base_ref[:, at] + STEP * fit_ref[:, at] + acc[r] * factor_ref[0:1, at]
        out = pltpu.make_async_copy(scratch[0], outs[0], sems.at[0])
        out.start()
        out.wait()

    (pre,) = graph_call(
        0,
        tasks,
        steps,
        own,
        similarity,
        [base, fit, factor],
        finish,
        [shape((k, wide), F32)],
        [pltpu.VMEM((k, wide), F32)],
        1,
        "next_own",
    )
    return pre


def hand_on(r, value, order_ref, ends_ref, outs, scratch, sems):
    out_ref, own_ref, send_ref = outs
    out, own = scratch
    out[r] = value
    own[r] = value.astype(BF16)
    at = pl.ds(pl.multiple_of(r * BS, BS), BS)

    def send(j, carry):
        pltpu.make_async_copy(own.at[r], send_ref.at[order_ref[j]], sems.at[0]).start()
        return carry

    lax.fori_loop(jnp.where(r == 0, 0, ends_ref[jnp.maximum(r - 1, 0)]), ends_ref[r], send, 0)
    pltpu.make_async_copy(own.at[r], own_ref.at[r], sems.at[1]).start()
    pltpu.make_async_copy(out.at[r], out_ref.at[:, at], sems.at[2]).start()


def handed(outs, sems):
    out_ref, own_ref, send_ref = outs
    wait_all(send_ref, sems.at[0])
    wait_all(own_ref, sems.at[1])
    wait_all(out_ref, sems.at[2])


def next_far(tasks, steps, recv, similarity, pre, factor, order, ends):
    rows = similarity.shape[0]
    wide = rows * BS
    k = recv.shape[1]

    def each_row(r, acc, extra, outs, scratch, sems):
        pre_ref, factor_ref, order_ref, ends_ref = extra
        at = pl.ds(pl.multiple_of(r * BS, BS), BS)
        value = shrink(pre_ref[:, at] + acc[r] * factor_ref[0:1, at])
        hand_on(r, value, order_ref, ends_ref, outs, scratch, sems)

    def finish(acc, extra, outs, scratch, sems):
        handed(outs, sems)

    return graph_call(
        1,
        tasks,
        steps,
        recv,
        similarity,
        [pre, factor, order, ends],
        finish,
        [shape((k, wide), F32), shape((rows, k, BS), BF16), shape(recv.shape, BF16)],
        [pltpu.VMEM((rows, k, BS), F32), pltpu.VMEM((rows, k, BS), BF16)],
        3,
        "next_far",
        each_row,
    )


def last_far(tasks, steps, recv, similarity, pre, factor, out_rows):
    rows = similarity.shape[0]
    wide = rows * BS

    def each_row(r, acc, extra, outs, scratch, sems):
        pre_ref, factor_ref = extra
        (out,) = scratch
        at = pl.ds(pl.multiple_of(r * BS, BS), BS)
        value = shrink(pre_ref[:, at] + acc[r] * factor_ref[0:1, at])
        out[r] = value[:out_rows]
        pltpu.make_async_copy(out.at[r], outs[0].at[:, at], sems.at[r]).start()

    def finish(acc, extra, outs, scratch, sems):
        for r in range(rows):
            at = slice(r * BS, (r + 1) * BS)
            pltpu.make_async_copy(scratch[0].at[r], outs[0].at[:, at], sems.at[r]).wait()

    (coeffs,) = graph_call(
        1,
        tasks,
        steps,
        recv,
        similarity,
        [pre, factor],
        finish,
        [shape((out_rows, wide), F32)],
        [pltpu.VMEM((rows, out_rows, BS), F32)],
        rows,
        "last_far",
        each_row,
    )
    return coeffs


def finish_first(mixed, fit, sources, first, weights, halves, pieces, order, ends):
    k, wide = mixed.shape
    blocks = wide // BS
    fetched = order.shape[0]
    count = len(pieces)
    dirs = weights.shape[2]
    group = 4

    def body(order_ref, ends_ref, source_ref, weights_ref, mixed_ref, fit_ref, *refs):
        out_ref, own_ref, send_ref, fit_out, mix, part, out, own, load_sems, sems, *buffers = refs[count:]
        loads = fit_loads(halves, pieces, refs, buffers, load_sems)
        loads.append(pltpu.make_async_copy(mixed_ref, mix, sems.at[3]))
        loads.append(pltpu.make_async_copy(fit_ref, part, sems.at[4]))
        for load in loads:
            load.start()
        for load in loads:
            load.wait()
        outs = (out_ref, own_ref, send_ref)
        for r in range(0, blocks, group):
            at = slice(r * BS, (r + group) * BS)
            total = part[:, at] + add_fit(source_ref, weights_ref, buffers, first, at)
            part[:, at] = total
            value = shrink(mix[:, at] + STEP * total)
            for i in range(group):
                block = value[:, i * BS : (i + 1) * BS]
                hand_on(jnp.int32(r + i), block, order_ref, ends_ref, outs, (out, own), sems)
        keep = pltpu.make_async_copy(part, fit_out, sems.at[5])
        keep.start()
        handed(outs, sems)
        keep.wait()

    return pl.pallas_call(
        body,
        in_specs=[SM, SM, SM, VM, HBM, HBM] + [HBM] * count,
        out_specs=[HBM] * 4,
        out_shape=[
            shape((k, wide), F32),
            shape((blocks, k, BS), BF16),
            shape((fetched, k, BS), BF16),
            shape((k, wide), F32),
        ],
        scratch_shapes=[
            pltpu.VMEM((k, wide), F32),
            pltpu.VMEM((k, wide), F32),
            pltpu.VMEM((blocks, k, BS), F32),
            pltpu.VMEM((blocks, k, BS), BF16),
            pltpu.SemaphoreType.DMA((count,)),
            pltpu.SemaphoreType.DMA((6,)),
        ]
        + [pltpu.VMEM((dirs, wide), BF16)] * count,
        compiler_params=params(),
        cost_estimate=cost(1, 12 * k * wide),
        name="finish_first",
    )(order, ends, sources, weights, mixed, fit, *pieces)


def local(
    signal,
    response,
    sphere_basis,
    initial,
    similarity,
    neighbour_count,
    neighbour_index,
    fetch_list,
):
    coef_count = initial.shape[0]
    peers = lax.axis_size("vox")
    parts = lax.axis_size("dir")

    cores = 2
    chips = parts // cores
    me = lax.axis_index("dir").astype(jnp.int32)
    chip, core = me // cores, me % cores
    far_chips = (1, chips - 1, *range(2, chips - 1))
    around = [lax.rem(chip + d, chips) * cores for d in (*far_chips, 0)]
    targets = jnp.stack([x + y for x in around for y in (core, 1 - core)])
    *cut, mine = cut_signal(signal, targets, parts)
    over_z = [
        lax.ppermute(
            x, "dir", [(i, (i // cores + d) % chips * cores + i % cores) for i in range(parts)]
        )
        for x, d in zip(cut, far_chips)
    ]
    swap = [(i, i ^ 1) for i in range(parts)]
    near_swap = lax.ppermute(mine, "dir", swap)
    came = [lax.rem(chip + chips - d, chips) * cores for d in (0, *far_chips)]
    sources = [came[0] + core, came[0] + 1 - core]
    sources = jnp.stack(sources + [x + core for x in came[1:]] + [x + 1 - core for x in came[1:]])
    lists, steps, weights, gram, sphere, sphere_t = set_up(
        neighbour_count, neighbour_index, response, sphere_basis.T, parts, fetch_list.size
    )
    want = lax.all_to_all(
        fetch_list.reshape(peers, -1), "vox", split_axis=0, concat_axis=0, tiled=True
    )
    def exchange(send):
        moved = lax.all_to_all(
            send.reshape(peers, -1, BS), "vox", split_axis=0, concat_axis=0, tiled=True
        )
        return moved.reshape(send.shape)

    own, send, order, ends = first_pack(initial, want)
    recv = exchange(send)
    (base,) = local_terms([initial], gram, sphere, sphere_t)
    summed = first_own(lists, steps, own, similarity)
    near_z, base, summed = lax.optimization_barrier((over_z[:2], base, summed))
    swapped = [lax.ppermute(x, "dir", swap) for x in near_z]
    fit = early_fit(sources, weights, [0, 1, 0, 0], [mine, near_swap, *near_z])
    far_z, fit = lax.optimization_barrier((over_z[2:], fit))
    (mixed,), factor = first_far(lists, steps, recv, similarity, summed, [base])
    late = [*far_z, *swapped, *(lax.ppermute(x, "dir", swap) for x in far_z)]
    halves = [0] * len(far_z) + [1] * len(over_z)
    coeffs, own, send, fit = finish_first(mixed, fit, sources, 4, weights, halves, late, order, ends)
    for iteration in range(1, ITERS):
        recv = exchange(send)
        (base,) = local_terms([coeffs], gram, sphere, sphere_t)
        pre = next_own(lists, steps, own, similarity, base, fit, factor)
        if iteration < ITERS - 1:
            coeffs, own, send = next_far(lists, steps, recv, similarity, pre, factor, order, ends)
        else:
            coeffs = last_far(lists, steps, recv, similarity, pre, factor, coef_count)
    return coeffs


def solution(mesh):
    in_specs = (
        P("dir", "vox"),
        P(),
        P(),
        P(None, ("vox", "dir")),
        P(("vox", "dir"), None, None, None),
        P(("vox", "dir")),
        P(("vox", "dir"), None),
        P(("vox", "dir"), None, None),
    )
    out_specs = P(None, ("vox", "dir"))
    return jax.shard_map(local, mesh=mesh, in_specs=in_specs, out_specs=out_specs, check_vma=False)
```

```python
import jax
import jax.numpy as jnp
from jax import lax
from jax.experimental import pallas as pl
from jax.experimental.pallas import tpu as pltpu
from jax.sharding import PartitionSpec as P

ITERS = 3
STEP = 0.2
SMOOTH = 2.0
PENALTY = 0.1
THRESHOLD = 0.2 * 0.25
KP = 160
CHUNKS = (160,)
BS = 128
UNROLL = 16
AHEAD = 2
RING = 4
F32 = jnp.float32
BF16 = jnp.bfloat16
SM = pl.BlockSpec(memory_space=pltpu.SMEM)
HBM = pl.BlockSpec(memory_space=pltpu.HBM)
VM = pl.BlockSpec(memory_space=pltpu.VMEM)
ANY = pl.BlockSpec(memory_space=pl.ANY)


def params(mib=53):
    return pltpu.CompilerParams(vmem_limit_bytes=mib << 20)


def cost(flops, moved):
    return pl.CostEstimate(flops=int(flops), bytes_accessed=int(moved), transcendentals=0)


def shape(dims, kind):
    return jax.ShapeDtypeStruct(dims, kind)


def shrink(x):
    return x - jnp.clip(x, -THRESHOLD, THRESHOLD)


def cut_signal(signal, targets, parts):
    dirs, wide = signal.shape
    span = wide // parts
    count = targets.shape[0]
    pairs = count // 2

    def body(targets_ref, signal_ref, *rest):
        outs, (held, sems) = rest[:pairs], rest[pairs:]

        def load(i):
            at = pl.multiple_of(targets_ref[i] * span, span)
            return pltpu.make_async_copy(signal_ref.at[:, pl.ds(at, span)], held.at[i], sems.at[i])

        def store(i):
            half = pl.ds(i % 2 * span, span)
            return pltpu.make_async_copy(held.at[i], outs[i // 2].at[:, half], sems.at[count + i])

        for i in range(count):
            load(i).start()
        for i in range(count):
            load(i).wait()
            store(i).start()
        for i in range(count):
            store(i).wait()

    return pl.pallas_call(
        body,
        in_specs=[SM, HBM],
        out_specs=[HBM] * pairs,
        out_shape=[shape((dirs, 2 * span), BF16)] * pairs,
        scratch_shapes=[
            pltpu.VMEM((count, dirs, span), BF16),
            pltpu.SemaphoreType.DMA((2 * count,)),
        ],
        compiler_params=params(),
        cost_estimate=cost(1, 4 * dirs * wide),
        name="cut_signal",
    )(targets, signal)


def fit_loads(halves, pieces, refs, buffers, sems):
    loads = []
    for i, (x, ref, to) in enumerate(zip(pieces, refs, buffers)):
        span = to.shape[1]
        loads.append(pltpu.make_async_copy(ref.at[:, pl.ds(halves[i] * span, span)], to, sems.at[i]))
    return loads


def add_fit(source_ref, weights, pieces, first, at):
    total = None
    for i, piece in enumerate(pieces):
        part = jnp.dot(weights[source_ref[first + i]], piece[:, at], preferred_element_type=F32)
        total = part if total is None else total + part
    return total


def early_fit(sources, weights, halves, pieces):
    parts, k, dirs = weights.shape
    span = pieces[0].shape[1] // 2
    count = len(pieces)
    tile = 512

    def body(source_ref, weights_ref, *refs):
        out_ref, *buffers = refs[count:]
        out, load_sems, sems = buffers[count:]
        buffers = buffers[:count]
        loads = fit_loads(halves, pieces, refs, buffers, load_sems)
        for load in loads:
            load.start()
        for load in loads:
            load.wait()
        for c in range(0, span, tile):
            at = slice(c, c + tile)
            out[:, at] = add_fit(source_ref, weights_ref, buffers, 0, at)
        keep = pltpu.make_async_copy(out, out_ref, sems.at[0])
        keep.start()
        keep.wait()

    return pl.pallas_call(
        body,
        in_specs=[SM, VM] + [HBM] * count,
        out_specs=HBM,
        out_shape=shape((k, span), F32),
        scratch_shapes=[pltpu.VMEM((dirs, span), BF16)] * count
        + [
            pltpu.VMEM((k, span), F32),
            pltpu.SemaphoreType.DMA((count,)),
            pltpu.SemaphoreType.DMA((1,)),
        ],
        compiler_params=params(),
        cost_estimate=cost(2 * k * dirs * count * span, 2 * dirs * count * span),
        name="early_fit",
    )(sources, weights, *pieces)


def set_up(count, index, response, sphere_t, parts, fetched):
    rows, slots = index.shape
    coefs, ns = sphere_t.shape
    dirs = response.shape[1] // parts
    room = rows * (slots + 1) + 2 * UNROLL

    def body(count_ref, index_ref, response_ref, sphere_ref, list_ref, steps_ref, w_ref, g_ref, s_ref, st_ref):
        def row(r, carry):
            def slot(m, inner):
                n_own, n_far = inner
                c = index_ref[r, m]
                near = c < rows
                at = jnp.where(near, n_own, n_far + room)
                list_ref[at] = r + 32 * m + 1024 * jnp.where(near, c, c - rows)
                one = jnp.where(near, 1, 0)
                return n_own + one, n_far + (1 - one)

            n_own, n_far = lax.fori_loop(0, count_ref[r], slot, carry)
            list_ref[n_own] = r + 1024 * rows
            list_ref[n_far + room] = r + 1024 * fetched
            return n_own + (n_own & 1), n_far + (n_far & 1)

        zero = jnp.int32(0)
        n_own, n_far = lax.fori_loop(0, rows, row, (zero, zero))
        for i in range(2 * UNROLL):
            list_ref[n_own + i] = rows + 1024 * rows
            list_ref[n_far + room + i] = rows + 1024 * fetched
        step = 2 * UNROLL
        steps_ref[0] = (n_own + step - 1) // step
        steps_ref[1] = (n_far + step - 1) // step

        def taller(x):
            x = x.astype(F32)
            return jnp.concatenate([x, jnp.zeros((KP - coefs, x.shape[1]), F32)], axis=0)

        tall = taller(response_ref[...])
        for i in range(parts):
            w_ref[i] = tall[:, i * dirs : (i + 1) * dirs].astype(BF16)
        low = tall.astype(BF16)
        nt = (((1,), (1,)), ((), ()))
        g_ref[...] = lax.dot_general(low, low, nt, preferred_element_type=F32)
        sphere = taller(sphere_ref[...])
        st_ref[...] = sphere.astype(BF16)
        s_ref[...] = sphere.T.astype(BF16)

    return pl.pallas_call(
        body,
        in_specs=[SM, SM, VM, VM],
        out_specs=[SM, SM, VM, VM, VM, VM],
        out_shape=[
            shape((2 * room,), jnp.int32),
            shape((2,), jnp.int32),
            shape((parts, KP, dirs), BF16),
            shape((KP, KP), F32),
            shape((ns, KP), BF16),
            shape((KP, ns), BF16),
        ],
        compiler_params=params(),
        cost_estimate=cost(1, 16_000_000),
        name="set_up",
    )(count, index, response, sphere_t)


def send_blocks(want_ref, own, send_ref, sem):
    peers, cap = want_ref.shape
    for p in range(peers):
        for q in range(cap):
            pltpu.make_async_copy(own.at[want_ref[p, q]], send_ref.at[p * cap + q], sem).start()


def wait_all(ref, sem):
    pltpu.make_async_copy(ref, ref, sem).wait()


def first_pack(initial, want):
    rows, wide = initial.shape
    blocks = wide // BS
    peers, cap = want.shape

    def body(want_ref, initial_ref, own_ref, send_ref, order_ref, ends_ref, held, own, sems):
        load = pltpu.make_async_copy(initial_ref, held, sems.at[0])
        load.start()
        load.wait()
        for r in range(blocks):
            block = held[:, r * BS : (r + 1) * BS]
            block = jnp.concatenate([block, jnp.ones((KP - rows, BS), F32)], axis=0)
            own[r] = block.astype(BF16)
        send_blocks(want_ref, own, send_ref, sems.at[1])
        keep = pltpu.make_async_copy(own, own_ref, sems.at[2])
        keep.start()
        for r in range(blocks):
            ends_ref[r] = 0
        for p in range(peers):
            for q in range(cap):
                w = want_ref[p, q]
                ends_ref[w] = ends_ref[w] + 1
        before = jnp.int32(0)
        for r in range(blocks):
            here = ends_ref[r]
            ends_ref[r] = before
            before = before + here
        for p in range(peers):
            for q in range(cap):
                w = want_ref[p, q]
                at = ends_ref[w]
                order_ref[at] = p * cap + q
                ends_ref[w] = at + 1
        wait_all(send_ref, sems.at[1])
        keep.wait()

    return pl.pallas_call(
        body,
        in_specs=[SM, HBM],
        out_specs=[HBM, HBM, SM, SM],
        out_shape=[
            shape((blocks, KP, BS), BF16),
            shape((peers * cap, KP, BS), BF16),
            shape((peers * cap,), jnp.int32),
            shape((blocks,), jnp.int32),
        ],
        scratch_shapes=[
            pltpu.VMEM((rows, wide), F32),
            pltpu.VMEM((blocks, KP, BS), BF16),
            pltpu.SemaphoreType.DMA((3,)),
        ],
        compiler_params=params(),
        cost_estimate=cost(1, 4 * rows * wide + 2 * (blocks + peers * cap) * KP * BS),
        name="first_pack",
    )(want, initial)


def local_terms(pieces, gram, sphere, sphere_t):
    wide = pieces[0].shape[1]
    rows = sum(p.shape[0] for p in pieces)
    ns = sphere.shape[0]
    tile = 512

    def body(*refs):
        ins, (g_ref, s_ref, st_ref), outs = refs[: len(pieces)], refs[len(pieces) :][:3], refs[len(pieces) + 3 :]
        c = jnp.concatenate(
            [r[...] for r in ins] + ([jnp.zeros((KP - rows, tile), F32)] if rows < KP else []), axis=0
        )
        hi = c.astype(BF16)
        lo = (c - hi.astype(F32)).astype(BF16)
        g = g_ref[...]
        gh = g.astype(BF16)
        gl = (g - gh.astype(F32)).astype(BF16)
        fid = jnp.dot(gh, hi, preferred_element_type=F32)
        fid += jnp.dot(gh, lo, preferred_element_type=F32)
        fid += jnp.dot(gl, hi, preferred_element_type=F32)
        amplitude = jnp.dot(s_ref[...], hi, preferred_element_type=F32)
        negative = jnp.minimum(amplitude, 0.0).astype(BF16)
        pulled = jnp.dot(st_ref[...], negative, preferred_element_type=F32)
        value = c - STEP * (fid + SMOOTH * c + PENALTY * pulled)
        at = 0
        for ref, k in zip(outs, CHUNKS):
            ref[...] = value[at : at + k]
            at += k

    def whole(*dims):
        return pl.BlockSpec(dims, lambda i: (0,) * len(dims))

    return pl.pallas_call(
        body,
        grid=(wide // tile,),
        in_specs=[pl.BlockSpec((p.shape[0], tile), lambda i: (0, i)) for p in pieces]
        + [whole(KP, KP), whole(ns, KP), whole(KP, ns)],
        out_specs=[pl.BlockSpec((k, tile), lambda i: (0, i)) for k in CHUNKS],
        out_shape=[shape((k, wide), F32) for k in CHUNKS],
        compiler_params=params(),
        cost_estimate=cost(2 * wide * KP * (3 * KP + 2 * ns), 8 * KP * wide),
        name="local_terms",
    )(*pieces, gram, sphere, sphere_t)


def run_tasks(list_ref, start, steps, blocks_ref, sim_ref, acc_ref, ring, sems, before, loaded, finish_row):
    rows = sim_ref.shape[0]
    nt = (((1,), (1,)), ((), ()))
    wide = 2 * UNROLL

    def fetch(s):
        slot = lax.rem(s, RING)
        for u in range(wide):
            e = list_ref[start + s * wide + u]
            r = jnp.minimum(e & 31, rows - 1)
            to = ring.at[slot * wide + u]
            pltpu.make_async_copy(sim_ref.at[r, (e >> 5) & 31], to, sems.at[slot]).start()

    for s in range(AHEAD):

        @pl.when(s < steps)
        def _():
            fetch(jnp.int32(s))

    before()

    def step(s, done):
        slot = lax.rem(s, RING)

        @pl.when(s + AHEAD < steps)
        def _():
            fetch(s + AHEAD)

        wait_all(ring.at[pl.ds(slot * wide, wide)], sems.at[slot])
        made = []
        for u in range(0, wide, 2):
            e, f = list_ref[start + s * wide + u], list_ref[start + s * wide + u + 1]
            at = slot * wide + u
            left = jnp.concatenate([blocks_ref[e >> 10], blocks_ref[f >> 10]], axis=1)
            right = jnp.concatenate([ring[at], ring[at + 1]], axis=1)
            made.append((e & 31, lax.dot_general(left, right, nt, preferred_element_type=F32)))
        for r, d in made:
            acc_ref[r] = acc_ref[r] + d
        if finish_row is None:
            return done
        pl.when(s == 0)(loaded)
        complete = list_ref[start + (s + 1) * wide] & 31
        lax.fori_loop(done, complete, lambda r, c: finish_row(r), None)
        return complete

    done = lax.fori_loop(0, steps, step, jnp.int32(0))
    if finish_row is None:
        loaded()
        return
    pl.when(steps == 0)(loaded)
    lax.fori_loop(done, rows, lambda r, c: finish_row(r), None)


def graph_call(
    which, tasks, steps, blocks, similarity, extra, finish, out_shape, scratch, sems, name, each_row=None
):
    rows = similarity.shape[0]
    given, k, _ = blocks.shape
    loaded = [x for x in extra if x.dtype != jnp.int32]

    def body(tasks_ref, steps_ref, blocks_ref, sim_ref, *rest):
        extra_refs, rest = rest[: len(extra)], rest[len(extra) :]
        outs, rest = rest[: len(out_shape)], rest[len(out_shape) :]
        held, acc, ring, ring_sems, load_sems, *rest = rest
        buffers, rest = rest[: len(loaded)], rest[len(loaded) :]
        own_scratch, own_sems = rest[: len(scratch)], rest[len(scratch) :]
        first = pltpu.make_async_copy(blocks_ref, held.at[pl.ds(0, given)], load_sems.at[0])
        first.start()
        held[given] = jnp.zeros((k, BS), BF16)
        for r in range(rows + 1):
            acc[r] = jnp.zeros((k, BS), F32)
        loads, ready = [], []
        left = list(buffers)
        for x, ref in zip(extra, extra_refs):
            if x.dtype == jnp.int32:
                ready.append(ref)
                continue
            to = left.pop(0)
            ready.append(to)
            loads.append(pltpu.make_async_copy(ref, to, load_sems.at[len(loads) + 1]))

        def before():
            for load in loads:
                load.start()
            first.wait()

        def all_loaded():
            for load in loads:
                load.wait()

        given_on = (acc, ready, outs, own_scratch, own_sems[0])
        finish_row = None if each_row is None else lambda r: each_row(r, *given_on)
        start = which * (tasks.shape[0] // 2)
        run_tasks(
            tasks_ref, start, steps_ref[which], held, sim_ref, acc, ring, ring_sems, before, all_loaded, finish_row
        )
        finish(*given_on)

    return pl.pallas_call(
        body,
        in_specs=[SM, SM, ANY, HBM] + [SM if x.dtype == jnp.int32 else HBM for x in extra],
        out_specs=[HBM] * len(out_shape),
        out_shape=out_shape,
        scratch_shapes=[
            pltpu.VMEM((given + 1, k, BS), BF16),
            pltpu.VMEM((rows + 1, k, BS), F32),
            pltpu.VMEM((RING * 2 * UNROLL, BS, BS), BF16),
            pltpu.SemaphoreType.DMA((RING,)),
            pltpu.SemaphoreType.DMA((len(loaded) + 1,)),
        ]
        + [pltpu.VMEM(x.shape, x.dtype) for x in loaded]
        + scratch
        + [pltpu.SemaphoreType.DMA((sems,))],
        compiler_params=params(),
        cost_estimate=cost(2 * k * BS * BS * rows * 14, 8_000_000),
        name=name,
    )(tasks, steps, blocks, similarity, *extra)


def first_own(tasks, steps, own, similarity):
    rows = similarity.shape[0]
    k = own.shape[1]

    def finish(acc, extra, outs, scratch, sems):
        out = pltpu.make_async_copy(acc.at[pl.ds(0, rows)], outs[0], sems.at[0])
        out.start()
        out.wait()

    (summed,) = graph_call(
        0, tasks, steps, own, similarity, [], finish, [shape((rows, k, BS), F32)], [], 1, "first_own"
    )
    return summed


def first_far(tasks, steps, recv, similarity, summed, bases):
    rows = similarity.shape[0]
    wide = rows * BS

    def finish(acc, extra, outs, scratch, sems):
        sum_ref, *base_refs = extra
        for r in range(rows):
            at = slice(r * BS, (r + 1) * BS)
            total = acc[r] + sum_ref[r]
            factor = (STEP * SMOOTH) / total[KP - 1 : KP]
            total = total * factor
            low = 0
            for base_ref, to, k in zip(base_refs, scratch, CHUNKS):
                to[:, at] = base_ref[:, at] + total[low : low + k]
                low += k
            scratch[-1][:, at] = jnp.broadcast_to(factor, (8, BS))
        copies = [pltpu.make_async_copy(s, o, sems.at[i]) for i, (s, o) in enumerate(zip(scratch, outs))]
        for copy in copies:
            copy.start()
        for copy in copies:
            copy.wait()

    dims = [(k, wide) for k in CHUNKS] + [(8, wide)]
    *mixed, factor = graph_call(
        1,
        tasks,
        steps,
        recv,
        similarity,
        [summed, *bases],
        finish,
        [shape(d, F32) for d in dims],
        [pltpu.VMEM(d, F32) for d in dims],
        len(dims),
        "first_far",
    )
    return mixed, factor


def next_own(tasks, steps, own, similarity, base, fit, factor):
    rows = similarity.shape[0]
    wide = rows * BS
    k = own.shape[1]

    def finish(acc, extra, outs, scratch, sems):
        base_ref, fit_ref, factor_ref = extra
        for r in range(rows):
            at = slice(r * BS, (r + 1) * BS)
            scratch[0][:, at] = base_ref[:, at] + STEP * fit_ref[:, at] + acc[r] * factor_ref[0:1, at]
        out = pltpu.make_async_copy(scratch[0], outs[0], sems.at[0])
        out.start()
        out.wait()

    (pre,) = graph_call(
        0,
        tasks,
        steps,
        own,
        similarity,
        [base, fit, factor],
        finish,
        [shape((k, wide), F32)],
        [pltpu.VMEM((k, wide), F32)],
        1,
        "next_own",
    )
    return pre


def hand_on(r, value, order_ref, ends_ref, outs, scratch, sems):
    out_ref, own_ref, send_ref = outs
    out, own = scratch
    out[r] = value
    own[r] = value.astype(BF16)
    at = pl.ds(pl.multiple_of(r * BS, BS), BS)

    def send(j, carry):
        pltpu.make_async_copy(own.at[r], send_ref.at[order_ref[j]], sems.at[0]).start()
        return carry

    lax.fori_loop(jnp.where(r == 0, 0, ends_ref[jnp.maximum(r - 1, 0)]), ends_ref[r], send, 0)
    pltpu.make_async_copy(own.at[r], own_ref.at[r], sems.at[1]).start()
    pltpu.make_async_copy(out.at[r], out_ref.at[:, at], sems.at[2]).start()


def handed(outs, sems):
    out_ref, own_ref, send_ref = outs
    wait_all(send_ref, sems.at[0])
    wait_all(own_ref, sems.at[1])
    wait_all(out_ref, sems.at[2])


def next_far(tasks, steps, recv, similarity, pre, factor, order, ends):
    rows = similarity.shape[0]
    wide = rows * BS
    k = recv.shape[1]

    def each_row(r, acc, extra, outs, scratch, sems):
        pre_ref, factor_ref, order_ref, ends_ref = extra
        at = pl.ds(pl.multiple_of(r * BS, BS), BS)
        value = shrink(pre_ref[:, at] + acc[r] * factor_ref[0:1, at])
        hand_on(r, value, order_ref, ends_ref, outs, scratch, sems)

    def finish(acc, extra, outs, scratch, sems):
        handed(outs, sems)

    return graph_call(
        1,
        tasks,
        steps,
        recv,
        similarity,
        [pre, factor, order, ends],
        finish,
        [shape((k, wide), F32), shape((rows, k, BS), BF16), shape(recv.shape, BF16)],
        [pltpu.VMEM((rows, k, BS), F32), pltpu.VMEM((rows, k, BS), BF16)],
        3,
        "next_far",
        each_row,
    )


def last_far(tasks, steps, recv, similarity, pre, factor, out_rows):
    rows = similarity.shape[0]
    wide = rows * BS

    def each_row(r, acc, extra, outs, scratch, sems):
        pre_ref, factor_ref = extra
        (out,) = scratch
        at = pl.ds(pl.multiple_of(r * BS, BS), BS)
        value = shrink(pre_ref[:, at] + acc[r] * factor_ref[0:1, at])
        out[r] = value[:out_rows]
        pltpu.make_async_copy(out.at[r], outs[0].at[:, at], sems.at[r]).start()

    def finish(acc, extra, outs, scratch, sems):
        for r in range(rows):
            at = slice(r * BS, (r + 1) * BS)
            pltpu.make_async_copy(scratch[0].at[r], outs[0].at[:, at], sems.at[r]).wait()

    (coeffs,) = graph_call(
        1,
        tasks,
        steps,
        recv,
        similarity,
        [pre, factor],
        finish,
        [shape((out_rows, wide), F32)],
        [pltpu.VMEM((rows, out_rows, BS), F32)],
        rows,
        "last_far",
        each_row,
    )
    return coeffs


def finish_first(mixed, fit, sources, first, weights, halves, pieces, order, ends):
    k, wide = mixed.shape
    blocks = wide // BS
    fetched = order.shape[0]
    count = len(pieces)
    dirs = weights.shape[2]
    group = 4

    def body(order_ref, ends_ref, source_ref, weights_ref, mixed_ref, fit_ref, *refs):
        out_ref, own_ref, send_ref, fit_out, mix, part, out, own, load_sems, sems, *buffers = refs[count:]
        loads = fit_loads(halves, pieces, refs, buffers, load_sems)
        loads.append(pltpu.make_async_copy(mixed_ref, mix, sems.at[3]))
        loads.append(pltpu.make_async_copy(fit_ref, part, sems.at[4]))
        for load in loads:
            load.start()
        for load in loads:
            load.wait()
        outs = (out_ref, own_ref, send_ref)
        for r in range(0, blocks, group):
            at = slice(r * BS, (r + group) * BS)
            total = part[:, at] + add_fit(source_ref, weights_ref, buffers, first, at)
            part[:, at] = total
            value = shrink(mix[:, at] + STEP * total)
            for i in range(group):
                block = value[:, i * BS : (i + 1) * BS]
                hand_on(jnp.int32(r + i), block, order_ref, ends_ref, outs, (out, own), sems)
        keep = pltpu.make_async_copy(part, fit_out, sems.at[5])
        keep.start()
        handed(outs, sems)
        keep.wait()

    return pl.pallas_call(
        body,
        in_specs=[SM, SM, SM, VM, HBM, HBM] + [HBM] * count,
        out_specs=[HBM] * 4,
        out_shape=[
            shape((k, wide), F32),
            shape((blocks, k, BS), BF16),
            shape((fetched, k, BS), BF16),
            shape((k, wide), F32),
        ],
        scratch_shapes=[
            pltpu.VMEM((k, wide), F32),
            pltpu.VMEM((k, wide), F32),
            pltpu.VMEM((blocks, k, BS), F32),
            pltpu.VMEM((blocks, k, BS), BF16),
            pltpu.SemaphoreType.DMA((count,)),
            pltpu.SemaphoreType.DMA((6,)),
        ]
        + [pltpu.VMEM((dirs, wide), BF16)] * count,
        compiler_params=params(),
        cost_estimate=cost(1, 12 * k * wide),
        name="finish_first",
    )(order, ends, sources, weights, mixed, fit, *pieces)


def local(
    signal,
    response,
    sphere_basis,
    initial,
    similarity,
    neighbour_count,
    neighbour_index,
    fetch_list,
):
    coef_count = initial.shape[0]
    peers = lax.axis_size("vox")
    parts = lax.axis_size("dir")

    cores = 2
    chips = parts // cores
    me = lax.axis_index("dir").astype(jnp.int32)
    chip, core = me // cores, me % cores
    far_chips = (1, chips - 1, *range(2, chips - 1))
    around = [lax.rem(chip + d, chips) * cores for d in (*far_chips, 0)]
    targets = jnp.stack([x + y for x in around for y in (core, 1 - core)])
    *cut, mine = cut_signal(signal, targets, parts)
    over_z = [
        lax.ppermute(
            x, "dir", [(i, (i // cores + d) % chips * cores + i % cores) for i in range(parts)]
        )
        for x, d in zip(cut, far_chips)
    ]
    swap = [(i, i ^ 1) for i in range(parts)]
    near_swap = lax.ppermute(mine, "dir", swap)
    came = [lax.rem(chip + chips - d, chips) * cores for d in (0, *far_chips)]
    sources = [came[0] + core, came[0] + 1 - core]
    sources = jnp.stack(sources + [x + core for x in came[1:]] + [x + 1 - core for x in came[1:]])
    lists, steps, weights, gram, sphere, sphere_t = set_up(
        neighbour_count, neighbour_index, response, sphere_basis.T, parts, fetch_list.size
    )
    want = lax.all_to_all(
        fetch_list.reshape(peers, -1), "vox", split_axis=0, concat_axis=0, tiled=True
    )
    def exchange(send):
        moved = lax.all_to_all(
            send.reshape(peers, -1, BS), "vox", split_axis=0, concat_axis=0, tiled=True
        )
        return moved.reshape(send.shape)

    own, send, order, ends = first_pack(initial, want)
    recv = exchange(send)
    (base,) = local_terms([initial], gram, sphere, sphere_t)
    summed = first_own(lists, steps, own, similarity)
    near_z, base, summed = lax.optimization_barrier((over_z[:2], base, summed))
    swapped = [lax.ppermute(x, "dir", swap) for x in near_z]
    fit = early_fit(sources, weights, [0, 1, 0, 0], [mine, near_swap, *near_z])
    far_z, fit = lax.optimization_barrier((over_z[2:], fit))
    (mixed,), factor = first_far(lists, steps, recv, similarity, summed, [base])
    late = [*far_z, *swapped, *(lax.ppermute(x, "dir", swap) for x in far_z)]
    halves = [0] * len(far_z) + [1] * len(over_z)
    coeffs, own, send, fit = finish_first(mixed, fit, sources, 4, weights, halves, late, order, ends)
    for iteration in range(1, ITERS):
        recv = exchange(send)
        (base,) = local_terms([coeffs], gram, sphere, sphere_t)
        pre = next_own(lists, steps, own, similarity, base, fit, factor)
        if iteration < ITERS - 1:
            coeffs, own, send = next_far(lists, steps, recv, similarity, pre, factor, order, ends)
        else:
            coeffs = last_far(lists, steps, recv, similarity, pre, factor, coef_count)
    return coeffs


def solution(mesh):
    in_specs = (
        P("dir", "vox"),
        P(),
        P(),
        P(None, ("vox", "dir")),
        P(("vox", "dir"), None, None, None),
        P(("vox", "dir")),
        P(("vox", "dir"), None),
        P(("vox", "dir"), None, None),
    )
    out_specs = P(None, ("vox", "dir"))
    return jax.shard_map(local, mesh=mesh, in_specs=in_specs, out_specs=out_specs, check_vma=False)
```

```python
import jax
import jax.numpy as jnp
from jax import lax
from jax.experimental import pallas as pl
from jax.experimental.pallas import tpu as pltpu
from jax.sharding import PartitionSpec as P

ITERS = 3
STEP = 0.2
SMOOTH = 2.0
PENALTY = 0.1
THRESHOLD = 0.2 * 0.25
KP = 160
CHUNKS = (160,)
BS = 128
UNROLL = 8
AHEAD = 4
RING = 6
F32 = jnp.float32
BF16 = jnp.bfloat16
SM = pl.BlockSpec(memory_space=pltpu.SMEM)
HBM = pl.BlockSpec(memory_space=pltpu.HBM)
VM = pl.BlockSpec(memory_space=pltpu.VMEM)
ANY = pl.BlockSpec(memory_space=pl.ANY)


def params(mib=53):
    return pltpu.CompilerParams(vmem_limit_bytes=mib << 20)


def cost(flops, moved):
    return pl.CostEstimate(flops=int(flops), bytes_accessed=int(moved), transcendentals=0)


def shape(dims, kind):
    return jax.ShapeDtypeStruct(dims, kind)


def shrink(x):
    return x - jnp.clip(x, -THRESHOLD, THRESHOLD)


def cut_signal(signal, targets, parts):
    dirs, wide = signal.shape
    span = wide // parts
    count = targets.shape[0]
    pairs = count // 2

    def body(targets_ref, signal_ref, *rest):
        outs, (held, sems) = rest[:pairs], rest[pairs:]

        def load(i):
            at = pl.multiple_of(targets_ref[i] * span, span)
            return pltpu.make_async_copy(signal_ref.at[:, pl.ds(at, span)], held.at[i], sems.at[i])

        def store(i):
            half = pl.ds(i % 2 * span, span)
            return pltpu.make_async_copy(held.at[i], outs[i // 2].at[:, half], sems.at[count + i])

        for i in range(count):
            load(i).start()
        for i in range(count):
            load(i).wait()
            store(i).start()
        for i in range(count):
            store(i).wait()

    return pl.pallas_call(
        body,
        in_specs=[SM, HBM],
        out_specs=[HBM] * pairs,
        out_shape=[shape((dirs, 2 * span), BF16)] * pairs,
        scratch_shapes=[
            pltpu.VMEM((count, dirs, span), BF16),
            pltpu.SemaphoreType.DMA((2 * count,)),
        ],
        compiler_params=params(),
        cost_estimate=cost(1, 4 * dirs * wide),
        name="cut_signal",
    )(targets, signal)


def fit_loads(halves, pieces, refs, buffers, sems):
    loads = []
    for i, (x, ref, to) in enumerate(zip(pieces, refs, buffers)):
        span = to.shape[1]
        loads.append(pltpu.make_async_copy(ref.at[:, pl.ds(halves[i] * span, span)], to, sems.at[i]))
    return loads


def add_fit(source_ref, weights, pieces, first, at):
    total = None
    for i, piece in enumerate(pieces):
        part = jnp.dot(weights[source_ref[first + i]], piece[:, at], preferred_element_type=F32)
        total = part if total is None else total + part
    return total


def early_fit(sources, weights, halves, pieces):
    parts, k, dirs = weights.shape
    span = pieces[0].shape[1] // 2
    count = len(pieces)
    tile = 512

    def body(source_ref, weights_ref, *refs):
        out_ref, *buffers = refs[count:]
        out, load_sems, sems = buffers[count:]
        buffers = buffers[:count]
        loads = fit_loads(halves, pieces, refs, buffers, load_sems)
        for load in loads:
            load.start()
        for load in loads:
            load.wait()
        for c in range(0, span, tile):
            at = slice(c, c + tile)
            out[:, at] = add_fit(source_ref, weights_ref, buffers, 0, at)
        keep = pltpu.make_async_copy(out, out_ref, sems.at[0])
        keep.start()
        keep.wait()

    return pl.pallas_call(
        body,
        in_specs=[SM, VM] + [HBM] * count,
        out_specs=HBM,
        out_shape=shape((k, span), F32),
        scratch_shapes=[pltpu.VMEM((dirs, span), BF16)] * count
        + [
            pltpu.VMEM((k, span), F32),
            pltpu.SemaphoreType.DMA((count,)),
            pltpu.SemaphoreType.DMA((1,)),
        ],
        compiler_params=params(),
        cost_estimate=cost(2 * k * dirs * count * span, 2 * dirs * count * span),
        name="early_fit",
    )(sources, weights, *pieces)


def set_up(count, index, response, sphere_t, parts, fetched):
    rows, slots = index.shape
    coefs, ns = sphere_t.shape
    dirs = response.shape[1] // parts
    room = rows * (slots + 1) + 2 * UNROLL

    def body(count_ref, index_ref, response_ref, sphere_ref, list_ref, steps_ref, w_ref, g_ref, s_ref, st_ref):
        def row(r, carry):
            def slot(m, inner):
                n_own, n_far = inner
                c = index_ref[r, m]
                near = c < rows
                at = jnp.where(near, n_own, n_far + room)
                list_ref[at] = r + 32 * m + 1024 * jnp.where(near, c, c - rows)
                one = jnp.where(near, 1, 0)
                return n_own + one, n_far + (1 - one)

            n_own, n_far = lax.fori_loop(0, count_ref[r], slot, carry)
            list_ref[n_own] = r + 1024 * rows
            list_ref[n_far + room] = r + 1024 * fetched
            return n_own + (n_own & 1), n_far + (n_far & 1)

        zero = jnp.int32(0)
        n_own, n_far = lax.fori_loop(0, rows, row, (zero, zero))
        for i in range(2 * UNROLL):
            list_ref[n_own + i] = rows + 1024 * rows
            list_ref[n_far + room + i] = rows + 1024 * fetched
        step = 2 * UNROLL
        steps_ref[0] = (n_own + step - 1) // step
        steps_ref[1] = (n_far + step - 1) // step

        def taller(x):
            x = x.astype(F32)
            return jnp.concatenate([x, jnp.zeros((KP - coefs, x.shape[1]), F32)], axis=0)

        tall = taller(response_ref[...])
        for i in range(parts):
            w_ref[i] = tall[:, i * dirs : (i + 1) * dirs].astype(BF16)
        low = tall.astype(BF16)
        nt = (((1,), (1,)), ((), ()))
        g_ref[...] = lax.dot_general(low, low, nt, preferred_element_type=F32)
        sphere = taller(sphere_ref[...])
        st_ref[...] = sphere.astype(BF16)
        s_ref[...] = sphere.T.astype(BF16)

    return pl.pallas_call(
        body,
        in_specs=[SM, SM, VM, VM],
        out_specs=[SM, SM, VM, VM, VM, VM],
        out_shape=[
            shape((2 * room,), jnp.int32),
            shape((2,), jnp.int32),
            shape((parts, KP, dirs), BF16),
            shape((KP, KP), F32),
            shape((ns, KP), BF16),
            shape((KP, ns), BF16),
        ],
        compiler_params=params(),
        cost_estimate=cost(1, 16_000_000),
        name="set_up",
    )(count, index, response, sphere_t)


def send_blocks(want_ref, own, send_ref, sem):
    peers, cap = want_ref.shape
    for p in range(peers):
        for q in range(cap):
            pltpu.make_async_copy(own.at[want_ref[p, q]], send_ref.at[p * cap + q], sem).start()


def wait_all(ref, sem):
    pltpu.make_async_copy(ref, ref, sem).wait()


def first_pack(initial, want):
    rows, wide = initial.shape
    blocks = wide // BS
    peers, cap = want.shape

    def body(want_ref, initial_ref, own_ref, send_ref, order_ref, ends_ref, held, own, sems):
        load = pltpu.make_async_copy(initial_ref, held, sems.at[0])
        load.start()
        load.wait()
        for r in range(blocks):
            block = held[:, r * BS : (r + 1) * BS]
            block = jnp.concatenate([block, jnp.ones((KP - rows, BS), F32)], axis=0)
            own[r] = block.astype(BF16)
        send_blocks(want_ref, own, send_ref, sems.at[1])
        keep = pltpu.make_async_copy(own, own_ref, sems.at[2])
        keep.start()
        for r in range(blocks):
            ends_ref[r] = 0
        for p in range(peers):
            for q in range(cap):
                w = want_ref[p, q]
                ends_ref[w] = ends_ref[w] + 1
        before = jnp.int32(0)
        for r in range(blocks):
            here = ends_ref[r]
            ends_ref[r] = before
            before = before + here
        for p in range(peers):
            for q in range(cap):
                w = want_ref[p, q]
                at = ends_ref[w]
                order_ref[at] = p * cap + q
                ends_ref[w] = at + 1
        wait_all(send_ref, sems.at[1])
        keep.wait()

    return pl.pallas_call(
        body,
        in_specs=[SM, HBM],
        out_specs=[HBM, HBM, SM, SM],
        out_shape=[
            shape((blocks, KP, BS), BF16),
            shape((peers * cap, KP, BS), BF16),
            shape((peers * cap,), jnp.int32),
            shape((blocks,), jnp.int32),
        ],
        scratch_shapes=[
            pltpu.VMEM((rows, wide), F32),
            pltpu.VMEM((blocks, KP, BS), BF16),
            pltpu.SemaphoreType.DMA((3,)),
        ],
        compiler_params=params(),
        cost_estimate=cost(1, 4 * rows * wide + 2 * (blocks + peers * cap) * KP * BS),
        name="first_pack",
    )(want, initial)


def local_terms(pieces, gram, sphere, sphere_t):
    wide = pieces[0].shape[1]
    rows = sum(p.shape[0] for p in pieces)
    ns = sphere.shape[0]
    tile = 512

    def body(*refs):
        ins, (g_ref, s_ref, st_ref), outs = refs[: len(pieces)], refs[len(pieces) :][:3], refs[len(pieces) + 3 :]
        c = jnp.concatenate(
            [r[...] for r in ins] + ([jnp.zeros((KP - rows, tile), F32)] if rows < KP else []), axis=0
        )
        hi = c.astype(BF16)
        lo = (c - hi.astype(F32)).astype(BF16)
        g = g_ref[...]
        gh = g.astype(BF16)
        gl = (g - gh.astype(F32)).astype(BF16)
        fid = jnp.dot(gh, hi, preferred_element_type=F32)
        fid += jnp.dot(gh, lo, preferred_element_type=F32)
        fid += jnp.dot(gl, hi, preferred_element_type=F32)
        amplitude = jnp.dot(s_ref[...], hi, preferred_element_type=F32)
        negative = jnp.minimum(amplitude, 0.0).astype(BF16)
        pulled = jnp.dot(st_ref[...], negative, preferred_element_type=F32)
        value = c - STEP * (fid + SMOOTH * c + PENALTY * pulled)
        at = 0
        for ref, k in zip(outs, CHUNKS):
            ref[...] = value[at : at + k]
            at += k

    def whole(*dims):
        return pl.BlockSpec(dims, lambda i: (0,) * len(dims))

    return pl.pallas_call(
        body,
        grid=(wide // tile,),
        in_specs=[pl.BlockSpec((p.shape[0], tile), lambda i: (0, i)) for p in pieces]
        + [whole(KP, KP), whole(ns, KP), whole(KP, ns)],
        out_specs=[pl.BlockSpec((k, tile), lambda i: (0, i)) for k in CHUNKS],
        out_shape=[shape((k, wide), F32) for k in CHUNKS],
        compiler_params=params(),
        cost_estimate=cost(2 * wide * KP * (3 * KP + 2 * ns), 8 * KP * wide),
        name="local_terms",
    )(*pieces, gram, sphere, sphere_t)


def run_tasks(list_ref, start, steps, blocks_ref, sim_ref, acc_ref, ring, sems, before, loaded, finish_row):
    rows = sim_ref.shape[0]
    nt = (((1,), (1,)), ((), ()))
    wide = 2 * UNROLL

    def fetch(s):
        slot = lax.rem(s, RING)
        for u in range(wide):
            e = list_ref[start + s * wide + u]
            r = jnp.minimum(e & 31, rows - 1)
            to = ring.at[slot * wide + u]
            pltpu.make_async_copy(sim_ref.at[r, (e >> 5) & 31], to, sems.at[slot]).start()

    for s in range(AHEAD):

        @pl.when(s < steps)
        def _():
            fetch(jnp.int32(s))

    before()

    def step(s, done):
        slot = lax.rem(s, RING)

        @pl.when(s + AHEAD < steps)
        def _():
            fetch(s + AHEAD)

        wait_all(ring.at[pl.ds(slot * wide, wide)], sems.at[slot])
        made = []
        for u in range(0, wide, 2):
            e, f = list_ref[start + s * wide + u], list_ref[start + s * wide + u + 1]
            at = slot * wide + u
            left = jnp.concatenate([blocks_ref[e >> 10], blocks_ref[f >> 10]], axis=1)
            right = jnp.concatenate([ring[at], ring[at + 1]], axis=1)
            made.append((e & 31, lax.dot_general(left, right, nt, preferred_element_type=F32)))
        for r, d in made:
            acc_ref[r] = acc_ref[r] + d
        if finish_row is None:
            return done
        pl.when(s == 0)(loaded)
        complete = list_ref[start + (s + 1) * wide] & 31
        lax.fori_loop(done, complete, lambda r, c: finish_row(r), None)
        return complete

    done = lax.fori_loop(0, steps, step, jnp.int32(0))
    if finish_row is None:
        loaded()
        return
    pl.when(steps == 0)(loaded)
    lax.fori_loop(done, rows, lambda r, c: finish_row(r), None)


def graph_call(
    which, tasks, steps, blocks, similarity, extra, finish, out_shape, scratch, sems, name, each_row=None
):
    rows = similarity.shape[0]
    given, k, _ = blocks.shape
    loaded = [x for x in extra if x.dtype != jnp.int32]

    def body(tasks_ref, steps_ref, blocks_ref, sim_ref, *rest):
        extra_refs, rest = rest[: len(extra)], rest[len(extra) :]
        outs, rest = rest[: len(out_shape)], rest[len(out_shape) :]
        held, acc, ring, ring_sems, load_sems, *rest = rest
        buffers, rest = rest[: len(loaded)], rest[len(loaded) :]
        own_scratch, own_sems = rest[: len(scratch)], rest[len(scratch) :]
        first = pltpu.make_async_copy(blocks_ref, held.at[pl.ds(0, given)], load_sems.at[0])
        first.start()
        held[given] = jnp.zeros((k, BS), BF16)
        for r in range(rows + 1):
            acc[r] = jnp.zeros((k, BS), F32)
        loads, ready = [], []
        left = list(buffers)
        for x, ref in zip(extra, extra_refs):
            if x.dtype == jnp.int32:
                ready.append(ref)
                continue
            to = left.pop(0)
            ready.append(to)
            loads.append(pltpu.make_async_copy(ref, to, load_sems.at[len(loads) + 1]))

        def before():
            for load in loads:
                load.start()
            first.wait()

        def all_loaded():
            for load in loads:
                load.wait()

        given_on = (acc, ready, outs, own_scratch, own_sems[0])
        finish_row = None if each_row is None else lambda r: each_row(r, *given_on)
        start = which * (tasks.shape[0] // 2)
        run_tasks(
            tasks_ref, start, steps_ref[which], held, sim_ref, acc, ring, ring_sems, before, all_loaded, finish_row
        )
        finish(*given_on)

    return pl.pallas_call(
        body,
        in_specs=[SM, SM, ANY, HBM] + [SM if x.dtype == jnp.int32 else HBM for x in extra],
        out_specs=[HBM] * len(out_shape),
        out_shape=out_shape,
        scratch_shapes=[
            pltpu.VMEM((given + 1, k, BS), BF16),
            pltpu.VMEM((rows + 1, k, BS), F32),
            pltpu.VMEM((RING * 2 * UNROLL, BS, BS), BF16),
            pltpu.SemaphoreType.DMA((RING,)),
            pltpu.SemaphoreType.DMA((len(loaded) + 1,)),
        ]
        + [pltpu.VMEM(x.shape, x.dtype) for x in loaded]
        + scratch
        + [pltpu.SemaphoreType.DMA((sems,))],
        compiler_params=params(),
        cost_estimate=cost(2 * k * BS * BS * rows * 14, 8_000_000),
        name=name,
    )(tasks, steps, blocks, similarity, *extra)


def first_own(tasks, steps, own, similarity):
    rows = similarity.shape[0]
    k = own.shape[1]

    def finish(acc, extra, outs, scratch, sems):
        out = pltpu.make_async_copy(acc.at[pl.ds(0, rows)], outs[0], sems.at[0])
        out.start()
        out.wait()

    (summed,) = graph_call(
        0, tasks, steps, own, similarity, [], finish, [shape((rows, k, BS), F32)], [], 1, "first_own"
    )
    return summed


def first_far(tasks, steps, recv, similarity, summed, bases):
    rows = similarity.shape[0]
    wide = rows * BS

    def finish(acc, extra, outs, scratch, sems):
        sum_ref, *base_refs = extra
        for r in range(rows):
            at = slice(r * BS, (r + 1) * BS)
            total = acc[r] + sum_ref[r]
            factor = (STEP * SMOOTH) / total[KP - 1 : KP]
            total = total * factor
            low = 0
            for base_ref, to, k in zip(base_refs, scratch, CHUNKS):
                to[:, at] = base_ref[:, at] + total[low : low + k]
                low += k
            scratch[-1][:, at] = jnp.broadcast_to(factor, (8, BS))
        copies = [pltpu.make_async_copy(s, o, sems.at[i]) for i, (s, o) in enumerate(zip(scratch, outs))]
        for copy in copies:
            copy.start()
        for copy in copies:
            copy.wait()

    dims = [(k, wide) for k in CHUNKS] + [(8, wide)]
    *mixed, factor = graph_call(
        1,
        tasks,
        steps,
        recv,
        similarity,
        [summed, *bases],
        finish,
        [shape(d, F32) for d in dims],
        [pltpu.VMEM(d, F32) for d in dims],
        len(dims),
        "first_far",
    )
    return mixed, factor


def next_own(tasks, steps, own, similarity, base, fit, factor):
    rows = similarity.shape[0]
    wide = rows * BS
    k = own.shape[1]

    def finish(acc, extra, outs, scratch, sems):
        base_ref, fit_ref, factor_ref = extra
        for r in range(rows):
            at = slice(r * BS, (r + 1) * BS)
            scratch[0][:, at] = base_ref[:, at] + STEP * fit_ref[:, at] + acc[r] * factor_ref[0:1, at]
        out = pltpu.make_async_copy(scratch[0], outs[0], sems.at[0])
        out.start()
        out.wait()

    (pre,) = graph_call(
        0,
        tasks,
        steps,
        own,
        similarity,
        [base, fit, factor],
        finish,
        [shape((k, wide), F32)],
        [pltpu.VMEM((k, wide), F32)],
        1,
        "next_own",
    )
    return pre


def hand_on(r, value, order_ref, ends_ref, outs, scratch, sems):
    out_ref, own_ref, send_ref = outs
    out, own = scratch
    out[r] = value
    own[r] = value.astype(BF16)
    at = pl.ds(pl.multiple_of(r * BS, BS), BS)

    def send(j, carry):
        pltpu.make_async_copy(own.at[r], send_ref.at[order_ref[j]], sems.at[0]).start()
        return carry

    lax.fori_loop(jnp.where(r == 0, 0, ends_ref[jnp.maximum(r - 1, 0)]), ends_ref[r], send, 0)
    pltpu.make_async_copy(own.at[r], own_ref.at[r], sems.at[1]).start()
    pltpu.make_async_copy(out.at[r], out_ref.at[:, at], sems.at[2]).start()


def handed(outs, sems):
    out_ref, own_ref, send_ref = outs
    wait_all(send_ref, sems.at[0])
    wait_all(own_ref, sems.at[1])
    wait_all(out_ref, sems.at[2])


def next_far(tasks, steps, recv, similarity, pre, factor, order, ends):
    rows = similarity.shape[0]
    wide = rows * BS
    k = recv.shape[1]

    def each_row(r, acc, extra, outs, scratch, sems):
        pre_ref, factor_ref, order_ref, ends_ref = extra
        at = pl.ds(pl.multiple_of(r * BS, BS), BS)
        value = shrink(pre_ref[:, at] + acc[r] * factor_ref[0:1, at])
        hand_on(r, value, order_ref, ends_ref, outs, scratch, sems)

    def finish(acc, extra, outs, scratch, sems):
        handed(outs, sems)

    return graph_call(
        1,
        tasks,
        steps,
        recv,
        similarity,
        [pre, factor, order, ends],
        finish,
        [shape((k, wide), F32), shape((rows, k, BS), BF16), shape(recv.shape, BF16)],
        [pltpu.VMEM((rows, k, BS), F32), pltpu.VMEM((rows, k, BS), BF16)],
        3,
        "next_far",
        each_row,
    )


def last_far(tasks, steps, recv, similarity, pre, factor, out_rows):
    rows = similarity.shape[0]
    wide = rows * BS

    def each_row(r, acc, extra, outs, scratch, sems):
        pre_ref, factor_ref = extra
        (out,) = scratch
        at = pl.ds(pl.multiple_of(r * BS, BS), BS)
        value = shrink(pre_ref[:, at] + acc[r] * factor_ref[0:1, at])
        out[r] = value[:out_rows]
        pltpu.make_async_copy(out.at[r], outs[0].at[:, at], sems.at[r]).start()

    def finish(acc, extra, outs, scratch, sems):
        for r in range(rows):
            at = slice(r * BS, (r + 1) * BS)
            pltpu.make_async_copy(scratch[0].at[r], outs[0].at[:, at], sems.at[r]).wait()

    (coeffs,) = graph_call(
        1,
        tasks,
        steps,
        recv,
        similarity,
        [pre, factor],
        finish,
        [shape((out_rows, wide), F32)],
        [pltpu.VMEM((rows, out_rows, BS), F32)],
        rows,
        "last_far",
        each_row,
    )
    return coeffs


def finish_first(mixed, fit, sources, first, weights, halves, pieces, order, ends):
    k, wide = mixed.shape
    blocks = wide // BS
    fetched = order.shape[0]
    count = len(pieces)
    dirs = weights.shape[2]
    group = 4

    def body(order_ref, ends_ref, source_ref, weights_ref, mixed_ref, fit_ref, *refs):
        out_ref, own_ref, send_ref, fit_out, mix, part, out, own, load_sems, sems, *buffers = refs[count:]
        loads = fit_loads(halves, pieces, refs, buffers, load_sems)
        loads.append(pltpu.make_async_copy(mixed_ref, mix, sems.at[3]))
        loads.append(pltpu.make_async_copy(fit_ref, part, sems.at[4]))
        for load in loads:
            load.start()
        for load in loads:
            load.wait()
        outs = (out_ref, own_ref, send_ref)
        for r in range(0, blocks, group):
            at = slice(r * BS, (r + group) * BS)
            total = part[:, at] + add_fit(source_ref, weights_ref, buffers, first, at)
            part[:, at] = total
            value = shrink(mix[:, at] + STEP * total)
            for i in range(group):
                block = value[:, i * BS : (i + 1) * BS]
                hand_on(jnp.int32(r + i), block, order_ref, ends_ref, outs, (out, own), sems)
        keep = pltpu.make_async_copy(part, fit_out, sems.at[5])
        keep.start()
        handed(outs, sems)
        keep.wait()

    return pl.pallas_call(
        body,
        in_specs=[SM, SM, SM, VM, HBM, HBM] + [HBM] * count,
        out_specs=[HBM] * 4,
        out_shape=[
            shape((k, wide), F32),
            shape((blocks, k, BS), BF16),
            shape((fetched, k, BS), BF16),
            shape((k, wide), F32),
        ],
        scratch_shapes=[
            pltpu.VMEM((k, wide), F32),
            pltpu.VMEM((k, wide), F32),
            pltpu.VMEM((blocks, k, BS), F32),
            pltpu.VMEM((blocks, k, BS), BF16),
            pltpu.SemaphoreType.DMA((count,)),
            pltpu.SemaphoreType.DMA((6,)),
        ]
        + [pltpu.VMEM((dirs, wide), BF16)] * count,
        compiler_params=params(),
        cost_estimate=cost(1, 12 * k * wide),
        name="finish_first",
    )(order, ends, sources, weights, mixed, fit, *pieces)


def local(
    signal,
    response,
    sphere_basis,
    initial,
    similarity,
    neighbour_count,
    neighbour_index,
    fetch_list,
):
    coef_count = initial.shape[0]
    peers = lax.axis_size("vox")
    parts = lax.axis_size("dir")

    cores = 2
    chips = parts // cores
    me = lax.axis_index("dir").astype(jnp.int32)
    chip, core = me // cores, me % cores
    far_chips = (1, chips - 1, *range(2, chips - 1))
    around = [lax.rem(chip + d, chips) * cores for d in (*far_chips, 0)]
    targets = jnp.stack([x + y for x in around for y in (core, 1 - core)])
    *cut, mine = cut_signal(signal, targets, parts)
    over_z = [
        lax.ppermute(
            x, "dir", [(i, (i // cores + d) % chips * cores + i % cores) for i in range(parts)]
        )
        for x, d in zip(cut, far_chips)
    ]
    swap = [(i, i ^ 1) for i in range(parts)]
    near_swap = lax.ppermute(mine, "dir", swap)
    came = [lax.rem(chip + chips - d, chips) * cores for d in (0, *far_chips)]
    sources = [came[0] + core, came[0] + 1 - core]
    sources = jnp.stack(sources + [x + core for x in came[1:]] + [x + 1 - core for x in came[1:]])
    lists, steps, weights, gram, sphere, sphere_t = set_up(
        neighbour_count, neighbour_index, response, sphere_basis.T, parts, fetch_list.size
    )
    want = lax.all_to_all(
        fetch_list.reshape(peers, -1), "vox", split_axis=0, concat_axis=0, tiled=True
    )
    def exchange(send):
        moved = lax.all_to_all(
            send.reshape(peers, -1, BS), "vox", split_axis=0, concat_axis=0, tiled=True
        )
        return moved.reshape(send.shape)

    own, send, order, ends = first_pack(initial, want)
    recv = exchange(send)
    (base,) = local_terms([initial], gram, sphere, sphere_t)
    summed = first_own(lists, steps, own, similarity)
    near_z, base, summed = lax.optimization_barrier((over_z[:2], base, summed))
    swapped = [lax.ppermute(x, "dir", swap) for x in near_z]
    fit = early_fit(sources, weights, [0, 1, 0, 0], [mine, near_swap, *near_z])
    far_z, fit = lax.optimization_barrier((over_z[2:], fit))
    (mixed,), factor = first_far(lists, steps, recv, similarity, summed, [base])
    late = [*far_z, *swapped, *(lax.ppermute(x, "dir", swap) for x in far_z)]
    halves = [0] * len(far_z) + [1] * len(over_z)
    coeffs, own, send, fit = finish_first(mixed, fit, sources, 4, weights, halves, late, order, ends)
    for iteration in range(1, ITERS):
        recv = exchange(send)
        (base,) = local_terms([coeffs], gram, sphere, sphere_t)
        pre = next_own(lists, steps, own, similarity, base, fit, factor)
        if iteration < ITERS - 1:
            coeffs, own, send = next_far(lists, steps, recv, similarity, pre, factor, order, ends)
        else:
            coeffs = last_far(lists, steps, recv, similarity, pre, factor, coef_count)
    return coeffs


def solution(mesh):
    in_specs = (
        P("dir", "vox"),
        P(),
        P(),
        P(None, ("vox", "dir")),
        P(("vox", "dir"), None, None, None),
        P(("vox", "dir")),
        P(("vox", "dir"), None),
        P(("vox", "dir"), None, None),
    )
    out_specs = P(None, ("vox", "dir"))
    return jax.shard_map(local, mesh=mesh, in_specs=in_specs, out_specs=out_specs, check_vma=False)
```
